128 devices in a mesh: tile: 8 (over x, core), gz: 16 (over y, z).
Axes of the slice: x: 4, y: 4, z: 4, core: 2. Of those that a mesh axis runs over, the one named last changes fastest.
Arguments:
- planes: bfloat16 [64, 3, 1024, 1024], P('gz', None, 'tile'), may hold values from -8 to 8
- level_gain: float32 [4], replicated, may hold values from 3 to 12
Outputs:
- joined: bfloat16 [3, 1024, 1024], P(None, ('tile', 'gz'))
The draws below stay inside these ranges and needn't reach their ends.
All inputs are finite; a program needn't handle non-finite values.
Results may differ from the reference program's by a relative error of at most 0.0068.
The reference program's roundings to bfloat16 on the way (of `luminance`) count: a program that leaves them out, or rounds other values in their place, can miss the bound.
Values may be sent and summed in bfloat16 or wider, within the bound.
A program may use at most 192 MiB of HBM per device.

```python
import math
import jax
import jax.numpy as jnp
from jax import lax

W = 1024
LEVELS = 4
Z = 64
H = 1024


def draw_planes(key, part):
    keys = jax.random.split(key, 10)
    low = jnp.log(0.3)
    high = jnp.log(1.5)
    row_amp = jnp.exp(jax.random.uniform(keys[1], (Z, 1, H, 1), jnp.float32, low, high))
    col_amp = jnp.exp(jax.random.uniform(keys[2], (Z, 1, 1, W), jnp.float32, low, high))
    noise = jax.random.normal(keys[0], (Z, 3, H, W), jnp.float32)
    values = noise * row_amp * col_amp
    values = jnp.clip(values, -8.0, 8.0)
    block_rows = H // 16
    block_cols = W // 16
    chosen = jax.random.uniform(keys[4], (block_rows, block_cols), jnp.float32) < 0.12
    first_plane = jax.random.randint(keys[5], (block_rows, block_cols), 0, Z)
    second_plane = (first_plane + 1 + jax.random.randint(keys[6], (block_rows, block_cols), 0, Z - 1)) % Z
    strength = jax.random.uniform(keys[7], (block_rows, block_cols), jnp.float32, 5.0, 7.0)
    lowered = strength * (1.0 - jax.random.uniform(keys[8], (block_rows, block_cols), jnp.float32, 0.004, 0.008))
    offsets = jax.random.uniform(keys[9], (Z, 3, 1, 1), jnp.float32, -1.0, 1.0)
    plane_ids = jnp.arange(Z, dtype=jnp.int32)[:, None, None]
    is_first = (plane_ids == first_plane[None]) & chosen[None]
    is_second = (plane_ids == second_plane[None]) & chosen[None]
    amplitude = jnp.where(is_first, strength[None], jnp.where(is_second, lowered[None], 0.0))
    amplitude = jnp.repeat(jnp.repeat(amplitude, 16, axis=1), 16, axis=2)
    active = jnp.repeat(jnp.repeat(is_first | is_second, 16, axis=1), 16, axis=2)
    row_ids = jnp.arange(H, dtype=jnp.int32)[:, None]
    col_ids = jnp.arange(W, dtype=jnp.int32)[None, :]
    checker = jnp.where((row_ids + col_ids) % 2 == 0, 1.0, -1.0).astype(jnp.float32)
    pattern = amplitude[:, None] * checker[None, None] + offsets
    values = jnp.where(active[:, None], pattern, values)
    return jnp.clip(values, -8.0, 8.0).astype(jnp.bfloat16)


def setup_inputs(seed: int = 0) -> dict:
    key_of = jax.random.split(jax.random.key(seed), 3)
    planes = draw_planes(jax.random.fold_in(key_of[2], 71), 0)
    level_gain = jnp.clip(jnp.exp(jax.random.uniform(key_of[1], (LEVELS,), jnp.float32, math.log(3.0), math.log(12.0))), 3.0, 12.0)
    return {"planes": planes, "level_gain": level_gain}


TAPS = (0.0625, 0.25, 0.375, 0.25, 0.0625)


def smooth_rows(field, stride):
    count = field.shape[0]
    padded = jnp.pad(field, ((2 * stride, 2 * stride), (0, 0)))
    result = jnp.zeros_like(field)
    for place, factor in enumerate(TAPS):
        result = result + factor * padded[place * stride: place * stride + count]
    return result


def smooth_cols(field, stride):
    count = field.shape[1]
    padded = jnp.pad(field, ((0, 0), (2 * stride, 2 * stride)))
    result = jnp.zeros_like(field)
    for place, factor in enumerate(TAPS):
        result = result + factor * padded[:, place * stride: place * stride + count]
    return result


def plane_energy(plane, level_gain):
    luminance = (0.299 * plane[0].astype(jnp.float32) + 0.587 * plane[1].astype(jnp.float32)
                 + 0.114 * plane[2].astype(jnp.float32)).astype(jnp.bfloat16)
    approx = lax.optimization_barrier(luminance).astype(jnp.float32)
    energy = jnp.zeros(approx.shape, jnp.float32)
    for level in range(LEVELS):
        stride = 2 ** level
        smoother = smooth_cols(smooth_rows(approx, stride), stride)
        detail = approx - smoother
        energy = energy + level_gain[level] * detail * detail
        approx = smoother
    return energy


def reference(planes, level_gain):
    scores = lax.map(lambda plane: plane_energy(plane, level_gain), planes)
    highest = jnp.max(scores, axis=0)

    def accumulate(carry, item):
        total, colour = carry
        score, plane = item
        weight = jnp.exp(score - highest)
        return (total + weight, colour + weight[None] * plane.astype(jnp.float32)), None

    start = (jnp.zeros(highest.shape, jnp.float32), jnp.zeros((3,) + highest.shape, jnp.float32))
    (total, colour), _ = lax.scan(accumulate, start, (scores, planes))
    return (colour / total[None]).astype(jnp.bfloat16)
```

```python
import jax
import jax.numpy as jnp
from jax import lax
from jax.experimental import pallas as pl
from jax.experimental.pallas import tpu as pltpu
from jax.sharding import PartitionSpec as P

LEVELS = 4


TAPS = (0.0625, 0.25, 0.375, 0.25, 0.0625)
SIDE = 4
HALF = 512


def extended_2(cells, sides, width):
    for axis, dim in sides:
        count = lax.axis_size(axis)
        ends = count - 1
        head = lax.slice_in_dim(cells, 0, width, axis=dim)
        tail = lax.slice_in_dim(cells, cells.shape[dim] - width, cells.shape[dim], axis=dim)
        cells = jnp.concatenate(
            [
                lax.ppermute(tail, axis, [(i, (i + 1) % count) for i in range(ends)]),
                cells,
                lax.ppermute(head, axis, [((i + 1) % count, i) for i in range(ends)]),
            ],
            axis=dim,
        )
    return cells


def taps_rows(field, stride):
    count = field.shape[1] - 4 * stride
    result = jnp.zeros((field.shape[0], count, field.shape[2]), jnp.float32)
    for place, factor in enumerate(TAPS):
        result = result + factor * field[:, place * stride : place * stride + count]
    return result


def smooth_cols(field, stride):
    count = field.shape[2]
    padded = jnp.pad(field, ((0, 0), (0, 0), (2 * stride, 2 * stride)))
    result = jnp.zeros_like(field)
    for place, factor in enumerate(TAPS):
        result = result + factor * padded[:, :, place * stride : place * stride + count]
    return result


def merged_states(logs, means):
    top = logs[0]
    for part in logs[1:]:
        top = jnp.maximum(top, part)
    weights = [jnp.exp(part - top) for part in logs]
    total = weights[0]
    for weight in weights[1:]:
        total = total + weight
    colours = []
    for channel in range(3):
        colour = weights[0] * means[0][channel]
        for weight, mean in zip(weights[1:], means[1:]):
            colour = colour + weight * mean[channel]
        colours.append(colour / total)
    return top, total, colours


def merge_kernel(
    logs_ref, means_ref, out_ref,
    logs_one, means_one, logs_two, means_two, logs_last, means_last,
    send_sems, recv_sems,
):
    place = lax.axis_index("gz")
    row = place // SIDE
    col = lax.rem(place, SIDE)

    def peer_of(half, step):
        if half == 0:
            return lax.rem(row + step, SIDE) * SIDE + col
        return row * SIDE + lax.rem(col + step, SIDE)

    barrier = pltpu.get_barrier_semaphore()
    for half in range(2):
        for step in range(1, SIDE):
            pl.semaphore_signal(
                barrier, inc=1, device_id={"gz": peer_of(half, step)},
                device_id_type=pl.DeviceIdType.MESH,
            )
    pl.semaphore_wait(barrier, 2 * (SIDE - 1))

    def view(ref, half, index):
        lanes = pl.ds(half * HALF, HALF)
        if half == 0:
            return ref.at[index, :, :, lanes] if len(ref.shape) == 4 else ref.at[index, :, :, :, lanes]
        return ref.at[:, index, :, lanes] if len(ref.shape) == 4 else ref.at[:, index, :, :, lanes]

    def remote(source, target, stage, half, step, kind, peer):
        return pltpu.make_async_remote_copy(
            src_ref=source, dst_ref=target,
            send_sem=send_sems.at[stage, half, step - 1, kind],
            recv_sem=recv_sems.at[stage, half, step - 1, kind],
            device_id={"gz": peer}, device_id_type=pl.DeviceIdType.MESH,
        )

    first = {}
    for step in (2, 1, 3):
        for half in range(2):
            axis_place = row if half == 0 else col
            index = lax.rem(axis_place + step, SIDE)
            peer = peer_of(half, step)
            pair = (
                remote(view(logs_ref, half, index), logs_one.at[half, step - 1], 0, half, step, 0, peer),
                remote(view(means_ref, half, index), means_one.at[half, step - 1], 0, half, step, 1, peer),
            )
            for copy in pair:
                copy.start()
            first[half, step] = pair

    for half in range(2):
        axis_place = row if half == 0 else col
        for step in range(1, SIDE):
            for copy in first[half, step]:
                copy.wait_recv()
        own_logs = view(logs_ref, half, axis_place)
        own_means = view(means_ref, half, axis_place)

        def body(block, carry, half=half, own_logs=own_logs, own_means=own_means):
            logs = [own_logs[block]] + [logs_one[half, k, block] for k in range(SIDE - 1)]
            means = [own_means[block].astype(jnp.float32)] + [
                means_one[half, k, block].astype(jnp.float32) for k in range(SIDE - 1)
            ]
            top, total, colours = merged_states(logs, means)
            logs_two[half, block] = top + jnp.log(total)
            for channel in range(3):
                means_two[half, block, channel] = colours[channel].astype(jnp.bfloat16)
            return carry

        lax.fori_loop(0, SIDE, body, 0)

    second = {}
    for half in range(2):
        axis_place = col if half == 0 else row
        for step in (2, 1, 3):
            index = lax.rem(axis_place + step, SIDE)
            peer = peer_of(1 - half, step)
            pair = (
                remote(logs_two.at[half, index], logs_last.at[half, step - 1], 1, half, step, 0, peer),
                remote(means_two.at[half, index], means_last.at[half, step - 1], 1, half, step, 1, peer),
            )
            for copy in pair:
                copy.start()
            second[half, step] = pair

    for half in range(2):
        axis_place = col if half == 0 else row
        for step in range(1, SIDE):
            for copy in second[half, step]:
                copy.wait_recv()
        logs = [logs_two[half, axis_place]] + [logs_last[half, k] for k in range(SIDE - 1)]
        means = [means_two[half, axis_place].astype(jnp.float32)] + [
            means_last[half, k].astype(jnp.float32) for k in range(SIDE - 1)
        ]
        _, _, colours = merged_states(logs, means)
        for channel in range(3):
            out_ref[channel, :, half * HALF : (half + 1) * HALF] = colours[channel].astype(jnp.bfloat16)

    for pair in list(first.values()) + list(second.values()):
        for copy in pair:
            copy.wait_send()


def merged_bands(logs, means):
    rows = logs.shape[2]
    return pl.pallas_call(
        merge_kernel,
        out_shape=jax.ShapeDtypeStruct((3, rows, 2 * HALF), jnp.bfloat16),
        in_specs=[pl.BlockSpec(memory_space=pltpu.VMEM)] * 2,
        out_specs=pl.BlockSpec(memory_space=pltpu.VMEM),
        scratch_shapes=[
            pltpu.VMEM((2, SIDE - 1, SIDE, rows, HALF), jnp.float32),
            pltpu.VMEM((2, SIDE - 1, SIDE, 3, rows, HALF), jnp.bfloat16),
            pltpu.VMEM((2, SIDE, rows, HALF), jnp.float32),
            pltpu.VMEM((2, SIDE, 3, rows, HALF), jnp.bfloat16),
            pltpu.VMEM((2, SIDE - 1, rows, HALF), jnp.float32),
            pltpu.VMEM((2, SIDE - 1, 3, rows, HALF), jnp.bfloat16),
            pltpu.SemaphoreType.DMA((2, 2, SIDE - 1, 2)),
            pltpu.SemaphoreType.DMA((2, 2, SIDE - 1, 2)),
        ],
        compiler_params=pltpu.CompilerParams(
            collective_id=0, has_side_effects=True, vmem_limit_bytes=32 * 1024 * 1024
        ),
    )(logs, means)


def per_device(planes, level_gain):
    rows = planes.shape[2]
    luminance = (
        0.299 * planes[:, 0].astype(jnp.float32)
        + 0.587 * planes[:, 1].astype(jnp.float32)
        + 0.114 * planes[:, 2].astype(jnp.float32)
    ).astype(jnp.bfloat16)
    reach = 2 * (2**LEVELS - 1)
    extended = extended_2(luminance, (("tile", 1),), reach)
    approx = extended.astype(jnp.float32)
    first_row = lax.axis_index("tile") * rows - reach
    image_rows = rows * lax.axis_size("tile")
    energy = jnp.zeros(approx.shape, jnp.float32)
    offset = 0
    for level in range(LEVELS):
        stride = 2**level
        smoother = smooth_cols(taps_rows(approx, stride), stride)
        offset = offset + 2 * stride
        global_row = first_row + offset + jnp.arange(smoother.shape[1], dtype=jnp.int32)
        inside = (global_row >= 0) & (global_row < image_rows)
        smoother = jnp.where(inside[None, :, None], smoother, 0.0)
        detail = approx[:, 2 * stride : -2 * stride] - smoother
        energy = energy[:, 2 * stride : -2 * stride] + level_gain[level] * detail * detail
        approx = smoother
    local_peak = jnp.max(energy, axis=0)
    weight = jnp.exp(energy - local_peak[None])
    total = jnp.sum(weight, axis=0)
    share = rows // lax.axis_size("gz")
    logs = (local_peak + jnp.log(total)).reshape(SIDE, SIDE, share, -1)
    means = jnp.stack(
        [
            jnp.sum(weight * planes[:, channel].astype(jnp.float32), axis=0) / total
            for channel in range(3)
        ]
    ).astype(jnp.bfloat16)
    means = means.reshape(3, SIDE, SIDE, share, -1).transpose(1, 2, 0, 3, 4)
    return merged_bands(logs, means)


def solution(mesh):
    return jax.shard_map(
        per_device,
        mesh=mesh,
        in_specs=(P("gz", None, "tile", None), P()),
        out_specs=P(None, ("tile", "gz"), None),
        check_vma=False,
    )
```

```python
import jax
import jax.numpy as jnp
import ml_dtypes
import numpy as np
from jax import lax
from jax.experimental import pallas as pl
from jax.experimental.pallas import tpu as pltpu
from jax.sharding import PartitionSpec as P

LEVELS = 4
TAPS = (0.0625, 0.25, 0.375, 0.25, 0.0625)
SIDE = 4
HALO = 32
LANES = 128
STEPS = (2, 1, 3)
CHAINS = {
    1: ((1, 16),),
    2: ((1, 17), (2, 16)),
    3: ((1, 19), (2, 18), (4, 16)),
    4: ((1, 23), (2, 22), (4, 20), (8, 16)),
}
UNROLL = 2


def column_weights(width):
    composed = np.eye(width)
    pieces = [[], [], []]
    tails = [[], [], []]
    blocks = (0, 1, width // LANES - 1)
    for level in range(LEVELS):
        smooth = np.zeros((width, width))
        for place, factor in enumerate(TAPS):
            smooth += factor * np.eye(width, k=(place - 2) * 2**level)
        composed = smooth @ composed
        scaled = np.pad(composed / 16.0 ** (level + 1), ((0, 0), (64, 64)))
        for variant, block in enumerate(blocks):
            window = scaled[block * LANES : (block + 1) * LANES, block * LANES : block * LANES + 256].T
            head = window.astype(ml_dtypes.bfloat16)
            pieces[variant].append(head)
            if level >= 2:
                tails[variant].append((window - head.astype(np.float64)).astype(ml_dtypes.bfloat16))
    return np.stack([np.concatenate(pieces[v] + tails[v], axis=1) for v in range(3)])


def merged_states(logs, means):
    top = logs[0]
    for part in logs[1:]:
        top = jnp.maximum(top, part)
    weights = [jnp.exp(part - top) for part in logs]
    total = weights[0]
    for weight in weights[1:]:
        total = total + weight
    colours = []
    for channel in range(3):
        colour = weights[0] * means[0][channel]
        for weight, mean in zip(weights[1:], means[1:]):
            colour = colour + weight * mean[channel]
        colours.append(colour / total)
    return top, total, colours


def eight(row):
    return pl.multiple_of(row * 8, 8)


def row_pass(source, target, stride, first, count, outputs):
    def body(index, carry):
        block = index // stride
        base = first + HALO + block * (stride * outputs) + (index - block * stride)
        cells = [source[pl.ds(eight(base + (j - 2) * stride), 8), :] for j in range(outputs + 4)]
        for _ in range(4):
            cells = [left + right for left, right in zip(cells[:-1], cells[1:])]
        for j in range(outputs):
            target[pl.ds(eight(base + j * stride), 8), :] = cells[j]
        return carry

    lax.fori_loop(0, count // outputs, body, 0, unroll=UNROLL)


def focus_kernel(
    gain_ref, planes_hbm, weights_hbm, out_ref,
    planes, weights, lum, field, smooth, buf_a, buf_b, score,
    logs_zero, means_zero, logs_one, means_one, logs_two, means_two, logs_last, means_last,
    load_sems, halo_send, halo_recv, send_sems, recv_sems,
):
    tile = lax.axis_index("tile")
    tiles = lax.axis_size("tile")
    place = lax.axis_index("gz")
    row = place // SIDE
    col = lax.rem(place, SIDE)
    rows = planes.shape[2]
    width = planes.shape[3]
    pairs = width // (2 * LANES)
    quarter = rows // SIDE
    extent = rows + 2 * HALO

    def peer_of(half, step):
        if half == 0:
            return lax.rem(row + step, SIDE) * SIDE + col
        return row * SIDE + lax.rem(col + step, SIDE)

    barrier = pltpu.get_barrier_semaphore()
    for half in range(2):
        for step in range(1, SIDE):
            pl.semaphore_signal(
                barrier, inc=1, device_id={"gz": peer_of(half, step)},
                device_id_type=pl.DeviceIdType.MESH,
            )

    @pl.when(tile > 0)
    def _():
        pl.semaphore_signal(
            barrier, inc=1, device_id={"tile": tile - 1}, device_id_type=pl.DeviceIdType.MESH
        )

    @pl.when(tile < tiles - 1)
    def _():
        pl.semaphore_signal(
            barrier, inc=1, device_id={"tile": tile + 1}, device_id_type=pl.DeviceIdType.MESH
        )

    loads = [
        pltpu.make_async_copy(
            planes_hbm.at[:, :, pl.ds(q * quarter, quarter), :],
            planes.at[:, :, pl.ds(q * quarter, quarter), :],
            load_sems.at[q],
        )
        for q in range(SIDE)
    ]
    weight_load = pltpu.make_async_copy(weights_hbm, weights, load_sems.at[SIDE])
    for q in (0, 3, 1, 2):
        loads[q].start()
    weight_load.start()

    def luminance(q):
        def body(index, carry):
            plane = index // 2
            start = pl.multiple_of(q * quarter + (index - plane * 2) * 16, 16)
            cells = [planes[plane, c, pl.ds(start, 16), :].astype(jnp.float32) for c in range(3)]
            value = (0.299 * cells[0] + 0.587 * cells[1] + 0.114 * cells[2]).astype(jnp.bfloat16)
            value = value.astype(jnp.float32)
            for k in range(width // LANES):
                field[k // 2, pl.ds(start * 8 + plane * 2 + k % 2, 16, stride=8), :] = value[
                    :, k * LANES : (k + 1) * LANES
                ]
            wide = jnp.concatenate([value, jnp.zeros((16, LANES), jnp.float32)], axis=1)
            wide = pltpu.roll(wide, LANES // 2, axis=1).astype(jnp.bfloat16)
            lum[plane, pl.ds(pl.multiple_of(start + HALO, 16), 16), :] = wide
            return carry

        lax.fori_loop(0, 8, body, 0)

    def halo_copy(side):
        source = HALO if side == 0 else rows
        target = HALO + rows if side == 0 else 0
        peer = tile - 1 if side == 0 else tile + 1
        return pltpu.make_async_remote_copy(
            src_ref=lum.at[:, pl.ds(source, HALO), :],
            dst_ref=lum.at[:, pl.ds(target, HALO), :],
            send_sem=halo_send.at[side], recv_sem=halo_recv.at[side],
            device_id={"tile": peer}, device_id_type=pl.DeviceIdType.MESH,
        )

    loads[0].wait()
    luminance(0)
    neighbours = jnp.where(tile > 0, 1, 0) + jnp.where(tile < tiles - 1, 1, 0)
    pl.semaphore_wait(barrier, 2 * (SIDE - 1) + neighbours)

    @pl.when(tile > 0)
    def _():
        halo_copy(0).start()

    @pl.when(tile == 0)
    def _():
        lum[:, 0:HALO, :] = jnp.zeros((SIDE, HALO, width + LANES), jnp.bfloat16)

    loads[3].wait()
    luminance(3)

    @pl.when(tile < tiles - 1)
    def _():
        halo_copy(1).start()

    @pl.when(tile == tiles - 1)
    def _():
        lum[:, HALO + rows : extent, :] = jnp.zeros((SIDE, HALO, width + LANES), jnp.bfloat16)

    for q in (1, 2):
        loads[q].wait()
        luminance(q)
    weight_load.wait()

    def columns(pair, spans):
        for k in range(2):
            block = pair * 2 + k
            variant = jnp.where(block == 0, 0, jnp.where(block == 2 * pairs - 1, 2, 1))
            window = pl.ds(pl.multiple_of(block * LANES, LANES), 2 * LANES)
            cells = jnp.concatenate(
                [
                    lum[plane, start : start + count, window]
                    for plane in range(SIDE)
                    for start, count in spans
                ],
                axis=0,
            )
            low = jnp.dot(cells, weights[variant, :, 0:256], preferred_element_type=jnp.float32)
            high = jnp.dot(
                cells, weights[variant, :, 256:512], preferred_element_type=jnp.float32
            ) + jnp.dot(cells, weights[variant, :, 512:768], preferred_element_type=jnp.float32)
            at = 0
            for plane in range(SIDE):
                for start, count in spans:
                    spot = pl.ds(start * 8 + plane * 2 + k, count, stride=8)
                    part = slice(at, at + count)
                    smooth[pair, 0, spot, :] = low[part, :LANES]
                    smooth[pair, 1, spot, :] = low[part, LANES:]
                    smooth[pair, 2, spot, :] = high[part, :LANES]
                    smooth[pair, 3, spot, :] = high[part, LANES:]
                    at += count

    def inner_columns(pair, carry):
        columns(pair, ((HALO, rows),))
        return carry

    lax.fori_loop(0, pairs, inner_columns, 0)

    @pl.when(tile < tiles - 1)
    def _():
        halo_copy(0).wait_recv()

    @pl.when(tile > 0)
    def _():
        halo_copy(1).wait_recv()

    def zero_outside(target, reach):
        blank = jnp.zeros((reach * 8, LANES), jnp.float32)

        @pl.when(tile == 0)
        def _():
            target[(HALO - reach) * 8 : HALO * 8, :] = blank

        @pl.when(tile == tiles - 1)
        def _():
            target[(HALO + rows) * 8 : (HALO + rows + reach) * 8, :] = blank

    def rows_smoothed(pair):
        for level in range(LEVELS, 0, -1):
            chain = CHAINS[level]
            reach = sum(2 * stride for stride, _ in chain)
            own = smooth.at[pair, level - 1]
            source = own
            for index, (stride, outputs) in enumerate(chain):
                reach -= 2 * stride
                target = (buf_a, buf_b)[index % 2]
                if index == level - 1 and level > 1:
                    target = own
                row_pass(source, target, stride, -reach, rows + 2 * reach, outputs)
                if reach:
                    zero_outside(target, reach)
                source = target

    gains = [gain_ref[level] for level in range(LEVELS)]

    def scored(pair):
        def body(block, carry):
            here = pl.ds(pl.multiple_of(block * 64, 64), 64)
            wide = pl.ds(pl.multiple_of(block * 64 + HALO * 8, 64), 64)
            approx = [field[pair, here, :], buf_a[wide, :]]
            approx += [smooth[pair, level, wide, :] for level in range(1, LEVELS)]
            energy = None
            for level in range(LEVELS):
                detail = approx[level] - approx[level + 1]
                term = gains[level] * (detail * detail)
                energy = term if energy is None else energy + term
            score[here, :] = energy
            return carry

        lax.fori_loop(0, rows // 8, body, 0)

    def states(pair):
        def body(block, carry):
            here = pl.ds(pl.multiple_of(block * 16, 16), 16)
            far = block // 2
            near = (block - far * 2) * 2
            for k in range(2):
                lanes = pl.ds(pl.multiple_of((pair * 2 + k) * LANES, LANES), LANES)
                parts = [
                    score[pl.ds(block * 128 + plane * 2 + k, 16, stride=8), :] for plane in range(SIDE)
                ]
                top = jnp.maximum(jnp.maximum(parts[0], parts[1]), jnp.maximum(parts[2], parts[3]))
                shares = [jnp.exp(part - top) for part in parts]
                total = (shares[0] + shares[1]) + (shares[2] + shares[3])
                inverse = 1.0 / total
                shares = [share * inverse for share in shares]
                log_sum = top + jnp.log(total)
                spots = ((far, near), (far, near + 1)) if k == 0 else ((near, far), (near + 1, far))
                for part, (first, second) in enumerate(spots):
                    logs_zero[pair, k, first, second] = log_sum[part * 8 : part * 8 + 8]
                for channel in range(3):
                    mean = shares[0] * planes[0, channel, here, lanes].astype(jnp.float32)
                    for plane in range(1, SIDE):
                        mean = mean + shares[plane] * planes[plane, channel, here, lanes].astype(
                            jnp.float32
                        )
                    mean = mean.astype(jnp.bfloat16)
                    for part, (first, second) in enumerate(spots):
                        means_zero[pair, k, first, second, channel] = mean[part * 8 : part * 8 + 8]
            return carry

        lax.fori_loop(0, rows // 16, body, 0)

    def first_copies(pair, half, step):
        index = lax.rem((row if half == 0 else col) + step, SIDE)
        return [
            pltpu.make_async_remote_copy(
                src_ref=source.at[pair, half, index], dst_ref=target.at[pair, half, step - 1],
                send_sem=send_sems.at[pair, half, step - 1, kind],
                recv_sem=recv_sems.at[pair, half, step - 1, kind],
                device_id={"gz": peer_of(half, step)}, device_id_type=pl.DeviceIdType.MESH,
            )
            for kind, (source, target) in enumerate(
                ((logs_zero, logs_one), (means_zero, means_one))
            )
        ]

    def first_merge(pair):
        for half in range(2):
            own = row if half == 0 else col
            for step in STEPS:
                for copy in first_copies(pair, half, step):
                    copy.wait_recv()

            def body(second, carry, half=half, own=own):
                logs = [logs_zero[pair, half, own, second]]
                logs += [logs_one[pair, half, k, second] for k in range(SIDE - 1)]
                means = [means_zero[pair, half, own, second].astype(jnp.float32)]
                means += [
                    means_one[pair, half, k, second].astype(jnp.float32) for k in range(SIDE - 1)
                ]
                top, total, colours = merged_states(logs, means)
                logs_two[half, second, pair] = top + jnp.log(total)
                for channel in range(3):
                    means_two[half, second, pair, channel] = colours[channel].astype(jnp.bfloat16)
                return carry

            lax.fori_loop(0, SIDE, body, 0)

    def one_pair(pair, carry):
        columns(pair, ((0, HALO), (HALO + rows, HALO)))
        rows_smoothed(pair)
        scored(pair)
        states(pair)
        for step in STEPS:
            for half in range(2):
                for copy in first_copies(pair, half, step):
                    copy.start()

        @pl.when(pair > 0)
        def _():
            first_merge(pair - 1)

        return carry

    lax.fori_loop(0, pairs, one_pair, 0)
    first_merge(pairs - 1)

    def last_copies(half, step):
        index = lax.rem((col if half == 0 else row) + step, SIDE)
        return [
            pltpu.make_async_remote_copy(
                src_ref=source.at[half, index], dst_ref=target.at[half, step - 1],
                send_sem=send_sems.at[pairs, half, step - 1, kind],
                recv_sem=recv_sems.at[pairs, half, step - 1, kind],
                device_id={"gz": peer_of(1 - half, step)}, device_id_type=pl.DeviceIdType.MESH,
            )
            for kind, (source, target) in enumerate(((logs_two, logs_last), (means_two, means_last)))
        ]

    for step in STEPS:
        for half in range(2):
            for copy in last_copies(half, step):
                copy.start()

    for half in range(2):
        own = col if half == 0 else row
        for step in STEPS:
            for copy in last_copies(half, step):
                copy.wait_recv()
        for pair in range(pairs):
            logs = [logs_two[half, own, pair]] + [logs_last[half, k, pair] for k in range(SIDE - 1)]
            means = [means_two[half, own, pair].astype(jnp.float32)]
            means += [means_last[half, k, pair].astype(jnp.float32) for k in range(SIDE - 1)]
            _, _, colours = merged_states(logs, means)
            lanes = slice((pair * 2 + half) * LANES, (pair * 2 + half + 1) * LANES)
            for channel in range(3):
                out_ref[channel, :, lanes] = colours[channel].astype(jnp.bfloat16)

    @pl.when(tile > 0)
    def _():
        halo_copy(0).wait_send()

    @pl.when(tile < tiles - 1)
    def _():
        halo_copy(1).wait_send()

    def drain(pair, carry):
        for half in range(2):
            for step in STEPS:
                for copy in first_copies(pair, half, step):
                    copy.wait_send()
        return carry

    lax.fori_loop(0, pairs, drain, 0)
    for half in range(2):
        for step in STEPS:
            for copy in last_copies(half, step):
                copy.wait_send()


def per_device(planes, level_gain):
    _, channels, rows, width = planes.shape
    share = rows // (SIDE * SIDE)
    pairs = width // (2 * LANES)
    extent = rows + 2 * HALO
    weights = jnp.asarray(column_weights(width))
    others = SIDE - 1
    return pl.pallas_call(
        focus_kernel,
        out_shape=jax.ShapeDtypeStruct((channels, share, width), jnp.bfloat16),
        in_specs=[
            pl.BlockSpec(memory_space=pltpu.SMEM),
            pl.BlockSpec(memory_space=pl.ANY),
            pl.BlockSpec(memory_space=pl.ANY),
        ],
        out_specs=pl.BlockSpec(memory_space=pltpu.VMEM),
        scratch_shapes=[
            pltpu.VMEM(planes.shape, jnp.bfloat16),
            pltpu.VMEM(weights.shape, jnp.bfloat16),
            pltpu.VMEM((SIDE, extent, width + LANES), jnp.bfloat16),
            pltpu.VMEM((pairs, rows * 8, LANES), jnp.float32),
            pltpu.VMEM((pairs, LEVELS, extent * 8, LANES), jnp.float32),
            pltpu.VMEM((extent * 8, LANES), jnp.float32),
            pltpu.VMEM((extent * 8, LANES), jnp.float32),
            pltpu.VMEM((rows * 8, LANES), jnp.float32),
            pltpu.VMEM((pairs, 2, SIDE, SIDE, share, LANES), jnp.float32),
            pltpu.VMEM((pairs, 2, SIDE, SIDE, channels, share, LANES), jnp.bfloat16),
            pltpu.VMEM((pairs, 2, others, SIDE, share, LANES), jnp.float32),
            pltpu.VMEM((pairs, 2, others, SIDE, channels, share, LANES), jnp.bfloat16),
            pltpu.VMEM((2, SIDE, pairs, share, LANES), jnp.float32),
            pltpu.VMEM((2, SIDE, pairs, channels, share, LANES), jnp.bfloat16),
            pltpu.VMEM((2, others, pairs, share, LANES), jnp.float32),
            pltpu.VMEM((2, others, pairs, channels, share, LANES), jnp.bfloat16),
            pltpu.SemaphoreType.DMA((SIDE + 1,)),
            pltpu.SemaphoreType.DMA((2,)),
            pltpu.SemaphoreType.DMA((2,)),
            pltpu.SemaphoreType.DMA((pairs + 1, 2, others, 2)),
            pltpu.SemaphoreType.DMA((pairs + 1, 2, others, 2)),
        ],
        compiler_params=pltpu.CompilerParams(
            collective_id=0, has_side_effects=True, vmem_limit_bytes=50 * 1024 * 1024
        ),
    )(level_gain, planes, weights)


def solution(mesh):
    return jax.shard_map(
        per_device,
        mesh=mesh,
        in_specs=(P("gz", None, "tile", None), P()),
        out_specs=P(None, ("tile", "gz"), None),
        check_vma=False,
    )
```

```python
import jax
import jax.numpy as jnp
import ml_dtypes
import numpy as np
from jax import lax
from jax.experimental import pallas as pl
from jax.experimental.pallas import tpu as pltpu
from jax.sharding import PartitionSpec as P

LEVELS = 4
TAPS = (0.0625, 0.25, 0.375, 0.25, 0.0625)
SIDE = 4
HALO = 32
LANES = 128
STEPS = (2, 1, 3)
CHAINS = {
    1: ((1, 16),),
    2: ((1, 17), (2, 16)),
    3: ((1, 19), (2, 18), (4, 16)),
    4: ((1, 23), (2, 22), (4, 20), (8, 16)),
}
UNROLL_LUM = 2
UNROLL_SCORE = 2
UNROLL_STATES = 2


def column_weights(width):
    composed = np.eye(width)
    pieces = [[], [], []]
    tails = [[], [], []]
    blocks = (0, 1, width // LANES - 1)
    for level in range(LEVELS):
        smooth = np.zeros((width, width))
        for place, factor in enumerate(TAPS):
            smooth += factor * np.eye(width, k=(place - 2) * 2**level)
        composed = smooth @ composed
        scaled = np.pad(composed / 16.0 ** (level + 1), ((0, 0), (64, 64)))
        for variant, block in enumerate(blocks):
            window = scaled[block * LANES : (block + 1) * LANES, block * LANES : block * LANES + 256].T
            head = window.astype(ml_dtypes.bfloat16)
            pieces[variant].append(head)
            if level >= 2:
                tails[variant].append((window - head.astype(np.float64)).astype(ml_dtypes.bfloat16))
    return np.stack([np.concatenate(pieces[v] + tails[v], axis=1) for v in range(3)])


def merged_states(logs, means):
    top = logs[0]
    for part in logs[1:]:
        top = jnp.maximum(top, part)
    weights = [jnp.exp(part - top) for part in logs]
    total = weights[0]
    for weight in weights[1:]:
        total = total + weight
    colours = []
    for channel in range(3):
        colour = weights[0] * means[0][channel]
        for weight, mean in zip(weights[1:], means[1:]):
            colour = colour + weight * mean[channel]
        colours.append(colour / total)
    return top, total, colours


def row_pass(source, target, stride, reach, rows, outputs, keep):
    for start in range(-reach, rows + reach, stride * outputs):
        for base in range(start, start + stride):
            at = [(base + HALO + (j - 2) * stride) * 8 for j in range(outputs + 4)]
            cells = [source[spot : spot + 8, :] for spot in at]
            for _ in range(4):
                cells = [left + right for left, right in zip(cells[:-1], cells[1:])]
            for j, cell in enumerate(cells):
                place = base + j * stride
                if place < 0:
                    cell = cell * keep[0]
                if place >= rows:
                    cell = cell * keep[1]
                target[at[j + 2] : at[j + 2] + 8, :] = cell


def focus_kernel(
    gain_ref, planes_hbm, weights_hbm, out_ref,
    planes, weights, lum, field, smooth, buf_a, buf_b, score,
    logs_zero, means_zero, logs_one, means_one, logs_two, means_two, logs_last, means_last,
    load_sems, halo_send, halo_recv, send_sems, recv_sems,
):
    tile = lax.axis_index("tile")
    tiles = lax.axis_size("tile")
    place = lax.axis_index("gz")
    row = place // SIDE
    col = lax.rem(place, SIDE)
    rows = planes.shape[2]
    width = planes.shape[3]
    pairs = width // (2 * LANES)
    quarter = rows // SIDE
    extent = rows + 2 * HALO

    def peer_of(half, step):
        if half == 0:
            return lax.rem(row + step, SIDE) * SIDE + col
        return row * SIDE + lax.rem(col + step, SIDE)

    barrier = pltpu.get_barrier_semaphore()
    for half in range(2):
        for step in range(1, SIDE):
            pl.semaphore_signal(
                barrier, inc=1, device_id={"gz": peer_of(half, step)},
                device_id_type=pl.DeviceIdType.MESH,
            )

    @pl.when(tile > 0)
    def _():
        pl.semaphore_signal(
            barrier, inc=1, device_id={"tile": tile - 1}, device_id_type=pl.DeviceIdType.MESH
        )

    @pl.when(tile < tiles - 1)
    def _():
        pl.semaphore_signal(
            barrier, inc=1, device_id={"tile": tile + 1}, device_id_type=pl.DeviceIdType.MESH
        )

    loads = [
        pltpu.make_async_copy(
            planes_hbm.at[:, :, pl.ds(q * quarter, quarter), :],
            planes.at[:, :, pl.ds(q * quarter, quarter), :],
            load_sems.at[q],
        )
        for q in range(SIDE)
    ]
    weight_load = pltpu.make_async_copy(weights_hbm, weights, load_sems.at[SIDE])
    for q in (0, 3, 1, 2):
        loads[q].start()
    weight_load.start()

    def luminance(q):
        def body(index, carry):
            plane = index // 2
            start = pl.multiple_of(q * quarter + (index - plane * 2) * 16, 16)
            cells = [planes[plane, c, pl.ds(start, 16), :].astype(jnp.float32) for c in range(3)]
            value = (0.299 * cells[0] + 0.587 * cells[1] + 0.114 * cells[2]).astype(jnp.bfloat16)
            value = value.astype(jnp.float32)
            for k in range(width // LANES):
                field[k // 2, pl.ds(start * 8 + plane * 2 + k % 2, 16, stride=8), :] = value[
                    :, k * LANES : (k + 1) * LANES
                ]
            wide = jnp.concatenate([value, jnp.zeros((16, LANES), jnp.float32)], axis=1)
            wide = pltpu.roll(wide, LANES // 2, axis=1).astype(jnp.bfloat16)
            lum[plane, pl.ds(pl.multiple_of(start + HALO, 16), 16), :] = wide
            return carry

        lax.fori_loop(0, 8, body, 0, unroll=UNROLL_LUM)

    def halo_copy(side):
        source = HALO if side == 0 else rows
        target = HALO + rows if side == 0 else 0
        peer = tile - 1 if side == 0 else tile + 1
        return pltpu.make_async_remote_copy(
            src_ref=lum.at[:, pl.ds(source, HALO), :],
            dst_ref=lum.at[:, pl.ds(target, HALO), :],
            send_sem=halo_send.at[side], recv_sem=halo_recv.at[side],
            device_id={"tile": peer}, device_id_type=pl.DeviceIdType.MESH,
        )

    loads[0].wait()
    luminance(0)
    neighbours = jnp.where(tile > 0, 1, 0) + jnp.where(tile < tiles - 1, 1, 0)
    pl.semaphore_wait(barrier, 2 * (SIDE - 1) + neighbours)

    @pl.when(tile > 0)
    def _():
        halo_copy(0).start()

    @pl.when(tile == 0)
    def _():
        lum[:, 0:HALO, :] = jnp.zeros((SIDE, HALO, width + LANES), jnp.bfloat16)

    loads[3].wait()
    luminance(3)

    @pl.when(tile < tiles - 1)
    def _():
        halo_copy(1).start()

    @pl.when(tile == tiles - 1)
    def _():
        lum[:, HALO + rows : extent, :] = jnp.zeros((SIDE, HALO, width + LANES), jnp.bfloat16)

    for q in (1, 2):
        loads[q].wait()
        luminance(q)
    weight_load.wait()

    def columns(pair, spans):
        for k in range(2):
            block = pair * 2 + k
            variant = jnp.where(block == 0, 0, jnp.where(block == 2 * pairs - 1, 2, 1))
            window = pl.ds(pl.multiple_of(block * LANES, LANES), 2 * LANES)
            cells = jnp.concatenate(
                [
                    lum[plane, start : start + count, window]
                    for plane in range(SIDE)
                    for start, count in spans
                ],
                axis=0,
            )
            low = jnp.dot(cells, weights[variant, :, 0:256], preferred_element_type=jnp.float32)
            high = jnp.dot(
                jnp.concatenate([cells, cells], axis=1),
                jnp.concatenate([weights[variant, :, 256:512], weights[variant, :, 512:768]], axis=0),
                preferred_element_type=jnp.float32,
            )
            at = 0
            for plane in range(SIDE):
                for start, count in spans:
                    spot = pl.ds(start * 8 + plane * 2 + k, count, stride=8)
                    part = slice(at, at + count)
                    smooth[pair, 0, spot, :] = low[part, :LANES]
                    smooth[pair, 1, spot, :] = low[part, LANES:]
                    smooth[pair, 2, spot, :] = high[part, :LANES]
                    smooth[pair, 3, spot, :] = high[part, LANES:]
                    at += count

    def inner_columns(pair, carry):
        columns(pair, ((HALO, rows),))
        return carry

    lax.fori_loop(0, pairs, inner_columns, 0)

    @pl.when(tile < tiles - 1)
    def _():
        halo_copy(0).wait_recv()

    @pl.when(tile > 0)
    def _():
        halo_copy(1).wait_recv()

    keep = (jnp.where(tile == 0, 0.0, 1.0), jnp.where(tile == tiles - 1, 0.0, 1.0))

    def rows_smoothed(pair):
        for level in range(LEVELS, 0, -1):
            chain = CHAINS[level]
            reach = sum(2 * stride for stride, _ in chain)
            own = smooth.at[pair, level - 1]
            source = own
            for index, (stride, outputs) in enumerate(chain):
                reach -= 2 * stride
                target = (buf_a, buf_b)[index % 2]
                if index == level - 1 and level > 1:
                    target = own
                row_pass(source, target, stride, reach, rows, outputs, keep)
                source = target

    gains = [gain_ref[level] for level in range(LEVELS)]

    def scored(pair):
        def body(block, carry):
            here = pl.ds(pl.multiple_of(block * 64, 64), 64)
            wide = pl.ds(pl.multiple_of(block * 64 + HALO * 8, 64), 64)
            approx = [field[pair, here, :], buf_a[wide, :]]
            approx += [smooth[pair, level, wide, :] for level in range(1, LEVELS)]
            energy = None
            for level in range(LEVELS):
                detail = approx[level] - approx[level + 1]
                term = gains[level] * (detail * detail)
                energy = term if energy is None else energy + term
            score[here, :] = energy
            return carry

        lax.fori_loop(0, rows // 8, body, 0, unroll=UNROLL_SCORE)

    def states(pair):
        def body(block, carry):
            here = pl.ds(pl.multiple_of(block * 16, 16), 16)
            far = block // 2
            near = (block - far * 2) * 2
            for k in range(2):
                lanes = pl.ds(pl.multiple_of((pair * 2 + k) * LANES, LANES), LANES)
                parts = [
                    score[pl.ds(block * 128 + plane * 2 + k, 16, stride=8), :] for plane in range(SIDE)
                ]
                top = jnp.maximum(jnp.maximum(parts[0], parts[1]), jnp.maximum(parts[2], parts[3]))
                shares = [jnp.exp(part - top) for part in parts]
                total = (shares[0] + shares[1]) + (shares[2] + shares[3])
                inverse = 1.0 / total
                shares = [share * inverse for share in shares]
                log_sum = top + jnp.log(total)
                spots = ((far, near), (far, near + 1)) if k == 0 else ((near, far), (near + 1, far))
                for part, (first, second) in enumerate(spots):
                    logs_zero[pair, k, first, second] = log_sum[part * 8 : part * 8 + 8]
                for channel in range(3):
                    mean = shares[0] * planes[0, channel, here, lanes].astype(jnp.float32)
                    for plane in range(1, SIDE):
                        mean = mean + shares[plane] * planes[plane, channel, here, lanes].astype(
                            jnp.float32
                        )
                    mean = mean.astype(jnp.bfloat16)
                    for part, (first, second) in enumerate(spots):
                        means_zero[pair, k, first, second, channel] = mean[part * 8 : part * 8 + 8]
            return carry

        lax.fori_loop(0, rows // 16, body, 0, unroll=UNROLL_STATES)

    def first_copies(pair, half, step):
        index = lax.rem((row if half == 0 else col) + step, SIDE)
        return [
            pltpu.make_async_remote_copy(
                src_ref=source.at[pair, half, index], dst_ref=target.at[pair, half, step - 1],
                send_sem=send_sems.at[pair, half, step - 1, kind],
                recv_sem=recv_sems.at[pair, half, step - 1, kind],
                device_id={"gz": peer_of(half, step)}, device_id_type=pl.DeviceIdType.MESH,
            )
            for kind, (source, target) in enumerate(
                ((logs_zero, logs_one), (means_zero, means_one))
            )
        ]

    def first_merge(pair):
        for half in range(2):
            own = row if half == 0 else col
            for step in STEPS:
                for copy in first_copies(pair, half, step):
                    copy.wait_recv()

            for second in range(SIDE):
                logs = [logs_zero[pair, half, own, second]]
                logs += [logs_one[pair, half, k, second] for k in range(SIDE - 1)]
                means = [means_zero[pair, half, own, second].astype(jnp.float32)]
                means += [
                    means_one[pair, half, k, second].astype(jnp.float32) for k in range(SIDE - 1)
                ]
                top, total, colours = merged_states(logs, means)
                logs_two[pair, half, second] = top + jnp.log(total)
                for channel in range(3):
                    means_two[pair, half, second, channel] = colours[channel].astype(jnp.bfloat16)

    def one_pair(pair, carry):
        columns(pair, ((0, HALO), (HALO + rows, HALO)))
        rows_smoothed(pair)
        scored(pair)
        states(pair)
        for step in STEPS:
            for half in range(2):
                for copy in first_copies(pair, half, step):
                    copy.start()

        @pl.when(pair > 1)
        def _():
            advance(pair - 2)

        return carry

    def advance(pair):
        first_merge(pair)
        for step in STEPS:
            for half in range(2):
                for copy in last_copies(pair, half, step):
                    copy.start()

    def last_copies(pair, half, step):
        index = lax.rem((col if half == 0 else row) + step, SIDE)
        return [
            pltpu.make_async_remote_copy(
                src_ref=source.at[pair, half, index], dst_ref=target.at[pair, half, step - 1],
                send_sem=send_sems.at[pairs + pair, half, step - 1, kind],
                recv_sem=recv_sems.at[pairs + pair, half, step - 1, kind],
                device_id={"gz": peer_of(1 - half, step)}, device_id_type=pl.DeviceIdType.MESH,
            )
            for kind, (source, target) in enumerate(((logs_two, logs_last), (means_two, means_last)))
        ]

    def last_merge(pair):
        for half in range(2):
            own = col if half == 0 else row
            for step in STEPS:
                for copy in last_copies(pair, half, step):
                    copy.wait_recv()
            logs = [logs_two[pair, half, own]] + [logs_last[pair, half, k] for k in range(SIDE - 1)]
            means = [means_two[pair, half, own].astype(jnp.float32)]
            means += [means_last[pair, half, k].astype(jnp.float32) for k in range(SIDE - 1)]
            _, _, colours = merged_states(logs, means)
            lanes = slice((pair * 2 + half) * LANES, (pair * 2 + half + 1) * LANES)
            for channel in range(3):
                out_ref[channel, :, lanes] = colours[channel].astype(jnp.bfloat16)

    lax.fori_loop(0, pairs, one_pair, 0)
    advance(pairs - 2)
    advance(pairs - 1)
    for pair in range(pairs):
        last_merge(pair)

    @pl.when(tile > 0)
    def _():
        halo_copy(0).wait_send()

    @pl.when(tile < tiles - 1)
    def _():
        halo_copy(1).wait_send()

    def drain(pair, carry):
        for half in range(2):
            for step in STEPS:
                for copy in first_copies(pair, half, step) + last_copies(pair, half, step):
                    copy.wait_send()
        return carry

    lax.fori_loop(0, pairs, drain, 0)


def per_device(planes, level_gain):
    _, channels, rows, width = planes.shape
    share = rows // (SIDE * SIDE)
    pairs = width // (2 * LANES)
    extent = rows + 2 * HALO
    weights = jnp.asarray(column_weights(width))
    others = SIDE - 1
    return pl.pallas_call(
        focus_kernel,
        out_shape=jax.ShapeDtypeStruct((channels, share, width), jnp.bfloat16),
        in_specs=[
            pl.BlockSpec(memory_space=pltpu.SMEM),
            pl.BlockSpec(memory_space=pl.ANY),
            pl.BlockSpec(memory_space=pl.ANY),
        ],
        out_specs=pl.BlockSpec(memory_space=pltpu.VMEM),
        scratch_shapes=[
            pltpu.VMEM(planes.shape, jnp.bfloat16),
            pltpu.VMEM(weights.shape, jnp.bfloat16),
            pltpu.VMEM((SIDE, extent, width + LANES), jnp.bfloat16),
            pltpu.VMEM((pairs, rows * 8, LANES), jnp.float32),
            pltpu.VMEM((pairs, LEVELS, extent * 8, LANES), jnp.float32),
            pltpu.VMEM((extent * 8, LANES), jnp.float32),
            pltpu.VMEM((extent * 8, LANES), jnp.float32),
            pltpu.VMEM((rows * 8, LANES), jnp.float32),
            pltpu.VMEM((pairs, 2, SIDE, SIDE, share, LANES), jnp.float32),
            pltpu.VMEM((pairs, 2, SIDE, SIDE, channels, share, LANES), jnp.bfloat16),
            pltpu.VMEM((pairs, 2, others, SIDE, share, LANES), jnp.float32),
            pltpu.VMEM((pairs, 2, others, SIDE, channels, share, LANES), jnp.bfloat16),
            pltpu.VMEM((pairs, 2, SIDE, share, LANES), jnp.float32),
            pltpu.VMEM((pairs, 2, SIDE, channels, share, LANES), jnp.bfloat16),
            pltpu.VMEM((pairs, 2, others, share, LANES), jnp.float32),
            pltpu.VMEM((pairs, 2, others, channels, share, LANES), jnp.bfloat16),
            pltpu.SemaphoreType.DMA((SIDE + 1,)),
            pltpu.SemaphoreType.DMA((2,)),
            pltpu.SemaphoreType.DMA((2,)),
            pltpu.SemaphoreType.DMA((2 * pairs, 2, others, 2)),
            pltpu.SemaphoreType.DMA((2 * pairs, 2, others, 2)),
        ],
        compiler_params=pltpu.CompilerParams(
            collective_id=0, has_side_effects=True, vmem_limit_bytes=60 * 1024 * 1024
        ),
    )(level_gain, planes, weights)


def solution(mesh):
    return jax.shard_map(
        per_device,
        mesh=mesh,
        in_specs=(P("gz", None, "tile", None), P()),
        out_specs=P(None, ("tile", "gz"), None),
        check_vma=False,
    )
```

```python
import jax
import jax.numpy as jnp
import ml_dtypes
import numpy as np
from jax import lax
from jax.experimental import pallas as pl
from jax.experimental.pallas import tpu as pltpu
from jax.sharding import PartitionSpec as P

LEVELS = 4
TAPS = (0.0625, 0.25, 0.375, 0.25, 0.0625)
SIDE = 4
HALO = 32
LANES = 128
STEPS = (2, 1, 3)
CHAINS = {
    1: ((1, 16),),
    2: ((1, 17), (2, 16)),
    3: ((1, 19), (2, 18), (4, 16)),
    4: ((1, 23), (2, 22), (4, 20), (8, 16)),
}
AHEAD = 3
UNROLL_LUM = 2
UNROLL_SCORE = 2
UNROLL_STATES = 2


def column_weights(width):
    composed = np.eye(width)
    pieces = [[], [], []]
    tails = [[], [], []]
    blocks = (0, 1, width // LANES - 1)
    for level in range(LEVELS):
        smooth = np.zeros((width, width))
        for place, factor in enumerate(TAPS):
            smooth += factor * np.eye(width, k=(place - 2) * 2**level)
        composed = smooth @ composed
        scaled = np.pad(composed / 16.0 ** (level + 1), ((0, 0), (64, 64)))
        for variant, block in enumerate(blocks):
            window = scaled[block * LANES : (block + 1) * LANES, block * LANES : block * LANES + 256].T
            head = window.astype(ml_dtypes.bfloat16)
            pieces[variant].append(head)
            if level >= 2:
                tails[variant].append((window - head.astype(np.float64)).astype(ml_dtypes.bfloat16))
    return np.stack([np.concatenate(pieces[v] + tails[v], axis=1) for v in range(3)])


def merged_states(logs, means):
    top = logs[0]
    for part in logs[1:]:
        top = jnp.maximum(top, part)
    weights = [jnp.exp(part - top) for part in logs]
    total = weights[0]
    for weight in weights[1:]:
        total = total + weight
    colours = []
    for channel in range(3):
        colour = weights[0] * means[0][channel]
        for weight, mean in zip(weights[1:], means[1:]):
            colour = colour + weight * mean[channel]
        colours.append(colour / total)
    return top, total, colours


def row_pass(source, target, stride, reach, rows, outputs, keep):
    for start in range(-reach, rows + reach, stride * outputs):
        for base in range(start, start + stride):
            at = [(base + HALO + (j - 2) * stride) * 8 for j in range(outputs + 4)]
            cells = [source[spot : spot + 8, :] for spot in at]
            for _ in range(4):
                cells = [left + right for left, right in zip(cells[:-1], cells[1:])]
            for j, cell in enumerate(cells):
                place = base + j * stride
                if place < 0:
                    cell = cell * keep[0]
                if place >= rows:
                    cell = cell * keep[1]
                target[at[j + 2] : at[j + 2] + 8, :] = cell


def focus_kernel(
    gain_ref, planes_hbm, weights_hbm, out_ref,
    planes, weights, lum, field, smooth_0, smooth_1, smooth_2, smooth_3, buf_a, buf_b, score,
    logs_zero, means_zero, logs_one, means_one, logs_two, means_two, logs_last, means_last,
    load_sems, halo_send, halo_recv, send_sems, recv_sems,
):
    smooths = (smooth_0, smooth_1, smooth_2, smooth_3)
    tile = lax.axis_index("tile")
    tiles = lax.axis_size("tile")
    place = lax.axis_index("gz")
    row = place // SIDE
    col = lax.rem(place, SIDE)
    rows = planes.shape[2]
    width = planes.shape[3]
    pairs = width // (2 * LANES)
    quarter = rows // SIDE
    extent = rows + 2 * HALO

    def peer_of(half, step):
        if half == 0:
            return lax.rem(row + step, SIDE) * SIDE + col
        return row * SIDE + lax.rem(col + step, SIDE)

    barrier = pltpu.get_barrier_semaphore()
    for half in range(2):
        for step in range(1, SIDE):
            pl.semaphore_signal(
                barrier, inc=1, device_id={"gz": peer_of(half, step)},
                device_id_type=pl.DeviceIdType.MESH,
            )

    @pl.when(tile > 0)
    def _():
        pl.semaphore_signal(
            barrier, inc=1, device_id={"tile": tile - 1}, device_id_type=pl.DeviceIdType.MESH
        )

    @pl.when(tile < tiles - 1)
    def _():
        pl.semaphore_signal(
            barrier, inc=1, device_id={"tile": tile + 1}, device_id_type=pl.DeviceIdType.MESH
        )

    loads = [
        pltpu.make_async_copy(
            planes_hbm.at[:, :, pl.ds(q * quarter, quarter), :],
            planes.at[:, :, pl.ds(q * quarter, quarter), :],
            load_sems.at[q],
        )
        for q in range(SIDE)
    ]
    weight_load = pltpu.make_async_copy(weights_hbm, weights, load_sems.at[SIDE])
    for q in (0, 3, 1, 2):
        loads[q].start()
    weight_load.start()

    def luminance(q):
        def body(index, carry):
            plane = index // 2
            start = pl.multiple_of(q * quarter + (index - plane * 2) * 16, 16)
            cells = [planes[plane, c, pl.ds(start, 16), :].astype(jnp.float32) for c in range(3)]
            value = (0.299 * cells[0] + 0.587 * cells[1] + 0.114 * cells[2]).astype(jnp.bfloat16)
            value = value.astype(jnp.float32)
            for k in range(width // LANES):
                field[k // 2, pl.ds(start * 8 + plane * 2 + k % 2, 16, stride=8), :] = value[
                    :, k * LANES : (k + 1) * LANES
                ]
            wide = jnp.concatenate([value, jnp.zeros((16, LANES), jnp.float32)], axis=1)
            wide = pltpu.roll(wide, LANES // 2, axis=1).astype(jnp.bfloat16)
            lum[plane, pl.ds(pl.multiple_of(start + HALO, 16), 16), :] = wide
            return carry

        lax.fori_loop(0, 8, body, 0, unroll=UNROLL_LUM)

    def halo_copy(side, part):
        source = HALO if side == 0 else rows
        target = HALO + rows if side == 0 else 0
        peer = tile - 1 if side == 0 else tile + 1
        first = 0 if part == 0 else (2 * part + 1) * LANES
        lanes = pl.ds(first, (2 * part + 3) * LANES - first)
        return pltpu.make_async_remote_copy(
            src_ref=lum.at[:, pl.ds(source, HALO), lanes],
            dst_ref=lum.at[:, pl.ds(target, HALO), lanes],
            send_sem=halo_send.at[side, part], recv_sem=halo_recv.at[side, part],
            device_id={"tile": peer}, device_id_type=pl.DeviceIdType.MESH,
        )

    loads[0].wait()
    luminance(0)
    neighbours = jnp.where(tile > 0, 1, 0) + jnp.where(tile < tiles - 1, 1, 0)
    pl.semaphore_wait(barrier, 2 * (SIDE - 1) + neighbours)

    @pl.when(tile > 0)
    def _():
        for part in range(pairs):
            halo_copy(0, part).start()

    @pl.when(tile == 0)
    def _():
        lum[:, 0:HALO, :] = jnp.zeros((SIDE, HALO, width + LANES), jnp.bfloat16)

    loads[3].wait()
    luminance(3)

    @pl.when(tile < tiles - 1)
    def _():
        for part in range(pairs):
            halo_copy(1, part).start()

    @pl.when(tile == tiles - 1)
    def _():
        lum[:, HALO + rows : extent, :] = jnp.zeros((SIDE, HALO, width + LANES), jnp.bfloat16)

    for q in (1, 2):
        loads[q].wait()
        luminance(q)
    weight_load.wait()

    def columns(pair, spans):
        for k in range(2):
            block = pair * 2 + k
            variant = 0 if block == 0 else 2 if block == 2 * pairs - 1 else 1
            window = pl.ds(block * LANES, 2 * LANES)
            smooth = smooths[pair]
            cells = jnp.concatenate(
                [
                    lum[plane, start : start + count, window]
                    for plane in range(SIDE)
                    for start, count in spans
                ],
                axis=0,
            )
            low = jnp.dot(cells, weights[variant, :, 0:256], preferred_element_type=jnp.float32)
            high = jnp.dot(
                jnp.concatenate([cells, cells], axis=1),
                jnp.concatenate([weights[variant, :, 256:512], weights[variant, :, 512:768]], axis=0),
                preferred_element_type=jnp.float32,
            )
            at = 0
            for plane in range(SIDE):
                for start, count in spans:
                    spot = pl.ds(start * 8 + plane * 2 + k, count, stride=8)
                    part = slice(at, at + count)
                    smooth[0, spot, :] = low[part, :LANES]
                    smooth[1, spot, :] = low[part, LANES:]
                    smooth[2, spot, :] = high[part, :LANES]
                    smooth[3, spot, :] = high[part, LANES:]
                    at += count

    inner = ((HALO, rows),)
    outer = ((0, HALO), (HALO + rows, HALO))
    for pair in range(AHEAD):
        columns(pair, inner)

    def outer_columns(pair):
        @pl.when(tile < tiles - 1)
        def _():
            halo_copy(0, pair).wait_recv()

        @pl.when(tile > 0)
        def _():
            halo_copy(1, pair).wait_recv()

        columns(pair, outer)

    keep = (jnp.where(tile == 0, 0.0, 1.0), jnp.where(tile == tiles - 1, 0.0, 1.0))

    def rows_smoothed(pair):
        for level in range(LEVELS, 0, -1):
            chain = CHAINS[level]
            reach = sum(2 * stride for stride, _ in chain)
            own = smooths[pair].at[level - 1]
            source = own
            for index, (stride, outputs) in enumerate(chain):
                reach -= 2 * stride
                target = (buf_a, buf_b)[index % 2]
                if index == level - 1 and level > 1:
                    target = own
                row_pass(source, target, stride, reach, rows, outputs, keep)
                source = target

    gains = [gain_ref[level] for level in range(LEVELS)]

    def scored(pair):
        def body(block, carry):
            here = pl.ds(pl.multiple_of(block * 64, 64), 64)
            wide = pl.ds(pl.multiple_of(block * 64 + HALO * 8, 64), 64)
            approx = [field[pair, here, :], buf_a[wide, :]]
            approx += [smooths[pair][level, wide, :] for level in range(1, LEVELS)]
            energy = None
            for level in range(LEVELS):
                detail = approx[level] - approx[level + 1]
                term = gains[level] * (detail * detail)
                energy = term if energy is None else energy + term
            score[here, :] = energy
            return carry

        lax.fori_loop(0, rows // 8, body, 0, unroll=UNROLL_SCORE)

    def states(pair):
        def body(block, carry):
            here = pl.ds(pl.multiple_of(block * 16, 16), 16)
            far = block // 2
            near = (block - far * 2) * 2
            for k in range(2):
                lanes = pl.ds(pl.multiple_of((pair * 2 + k) * LANES, LANES), LANES)
                parts = [
                    score[pl.ds(block * 128 + plane * 2 + k, 16, stride=8), :] for plane in range(SIDE)
                ]
                top = jnp.maximum(jnp.maximum(parts[0], parts[1]), jnp.maximum(parts[2], parts[3]))
                shares = [jnp.exp(part - top) for part in parts]
                total = (shares[0] + shares[1]) + (shares[2] + shares[3])
                inverse = 1.0 / total
                shares = [share * inverse for share in shares]
                log_sum = top + jnp.log(total)
                spots = ((far, near), (far, near + 1)) if k == 0 else ((near, far), (near + 1, far))
                for part, (first, second) in enumerate(spots):
                    logs_zero[pair, k, first, second] = log_sum[part * 8 : part * 8 + 8]
                for channel in range(3):
                    mean = shares[0] * planes[0, channel, here, lanes].astype(jnp.float32)
                    for plane in range(1, SIDE):
                        mean = mean + shares[plane] * planes[plane, channel, here, lanes].astype(
                            jnp.float32
                        )
                    mean = mean.astype(jnp.bfloat16)
                    for part, (first, second) in enumerate(spots):
                        means_zero[pair, k, first, second, channel] = mean[part * 8 : part * 8 + 8]
            return carry

        lax.fori_loop(0, rows // 16, body, 0, unroll=UNROLL_STATES)

    def first_copies(pair, half, step):
        index = lax.rem((row if half == 0 else col) + step, SIDE)
        return [
            pltpu.make_async_remote_copy(
                src_ref=source.at[pair, half, index], dst_ref=target.at[pair, half, step - 1],
                send_sem=send_sems.at[pair, half, step - 1, kind],
                recv_sem=recv_sems.at[pair, half, step - 1, kind],
                device_id={"gz": peer_of(half, step)}, device_id_type=pl.DeviceIdType.MESH,
            )
            for kind, (source, target) in enumerate(
                ((logs_zero, logs_one), (means_zero, means_one))
            )
        ]

    def first_merge(pair):
        for half in range(2):
            own = row if half == 0 else col
            for step in STEPS:
                for copy in first_copies(pair, half, step):
                    copy.wait_recv()

            for second in range(SIDE):
                logs = [logs_zero[pair, half, own, second]]
                logs += [logs_one[pair, half, k, second] for k in range(SIDE - 1)]
                means = [means_zero[pair, half, own, second].astype(jnp.float32)]
                means += [
                    means_one[pair, half, k, second].astype(jnp.float32) for k in range(SIDE - 1)
                ]
                top, total, colours = merged_states(logs, means)
                logs_two[pair, half, second] = top + jnp.log(total)
                for channel in range(3):
                    means_two[pair, half, second, channel] = colours[channel].astype(jnp.bfloat16)

    def one_pair(pair):
        if pair + AHEAD < pairs:
            columns(pair + AHEAD, inner)
        if pair + 1 < pairs:
            outer_columns(pair + 1)
        rows_smoothed(pair)
        scored(pair)
        states(pair)
        for step in STEPS:
            for half in range(2):
                for copy in first_copies(pair, half, step):
                    copy.start()

        if pair > 1:
            advance(pair - 2)

    def advance(pair):
        first_merge(pair)
        for step in STEPS:
            for half in range(2):
                for copy in last_copies(pair, half, step):
                    copy.start()

    def last_copies(pair, half, step):
        index = lax.rem((col if half == 0 else row) + step, SIDE)
        return [
            pltpu.make_async_remote_copy(
                src_ref=source.at[pair, half, index], dst_ref=target.at[pair, half, step - 1],
                send_sem=send_sems.at[pairs + pair, half, step - 1, kind],
                recv_sem=recv_sems.at[pairs + pair, half, step - 1, kind],
                device_id={"gz": peer_of(1 - half, step)}, device_id_type=pl.DeviceIdType.MESH,
            )
            for kind, (source, target) in enumerate(((logs_two, logs_last), (means_two, means_last)))
        ]

    def last_merge(pair):
        for half in range(2):
            own = col if half == 0 else row
            for step in STEPS:
                for copy in last_copies(pair, half, step):
                    copy.wait_recv()
            logs = [logs_two[pair, half, own]] + [logs_last[pair, half, k] for k in range(SIDE - 1)]
            means = [means_two[pair, half, own].astype(jnp.float32)]
            means += [means_last[pair, half, k].astype(jnp.float32) for k in range(SIDE - 1)]
            _, _, colours = merged_states(logs, means)
            lanes = slice((pair * 2 + half) * LANES, (pair * 2 + half + 1) * LANES)
            for channel in range(3):
                out_ref[channel, :, lanes] = colours[channel].astype(jnp.bfloat16)

    outer_columns(0)
    for pair in range(pairs):
        one_pair(pair)
    advance(pairs - 2)
    advance(pairs - 1)
    for pair in range(pairs):
        last_merge(pair)

    @pl.when(tile > 0)
    def _():
        for part in range(pairs):
            halo_copy(0, part).wait_send()

    @pl.when(tile < tiles - 1)
    def _():
        for part in range(pairs):
            halo_copy(1, part).wait_send()

    def drain(pair, carry):
        for half in range(2):
            for step in STEPS:
                for copy in first_copies(pair, half, step) + last_copies(pair, half, step):
                    copy.wait_send()
        return carry

    lax.fori_loop(0, pairs, drain, 0)


def per_device(planes, level_gain):
    _, channels, rows, width = planes.shape
    share = rows // (SIDE * SIDE)
    pairs = width // (2 * LANES)
    extent = rows + 2 * HALO
    weights = jnp.asarray(column_weights(width))
    others = SIDE - 1
    return pl.pallas_call(
        focus_kernel,
        out_shape=jax.ShapeDtypeStruct((channels, share, width), jnp.bfloat16),
        in_specs=[
            pl.BlockSpec(memory_space=pltpu.SMEM),
            pl.BlockSpec(memory_space=pl.ANY),
            pl.BlockSpec(memory_space=pl.ANY),
        ],
        out_specs=pl.BlockSpec(memory_space=pltpu.VMEM),
        scratch_shapes=[
            pltpu.VMEM(planes.shape, jnp.bfloat16),
            pltpu.VMEM(weights.shape, jnp.bfloat16),
            pltpu.VMEM((SIDE, extent, width + LANES), jnp.bfloat16),
            pltpu.VMEM((pairs, rows * 8, LANES), jnp.float32),
            pltpu.VMEM((LEVELS, extent * 8, LANES), jnp.float32),
            pltpu.VMEM((LEVELS, extent * 8, LANES), jnp.float32),
            pltpu.VMEM((LEVELS, extent * 8, LANES), jnp.float32),
            pltpu.VMEM((LEVELS, extent * 8, LANES), jnp.float32),
            pltpu.VMEM((extent * 8, LANES), jnp.float32),
            pltpu.VMEM((extent * 8, LANES), jnp.float32),
            pltpu.VMEM((rows * 8, LANES), jnp.float32),
            pltpu.VMEM((pairs, 2, SIDE, SIDE, share, LANES), jnp.float32),
            pltpu.VMEM((pairs, 2, SIDE, SIDE, channels, share, LANES), jnp.bfloat16),
            pltpu.VMEM((pairs, 2, others, SIDE, share, LANES), jnp.float32),
            pltpu.VMEM((pairs, 2, others, SIDE, channels, share, LANES), jnp.bfloat16),
            pltpu.VMEM((pairs, 2, SIDE, share, LANES), jnp.float32),
            pltpu.VMEM((pairs, 2, SIDE, channels, share, LANES), jnp.bfloat16),
            pltpu.VMEM((pairs, 2, others, share, LANES), jnp.float32),
            pltpu.VMEM((pairs, 2, others, channels, share, LANES), jnp.bfloat16),
            pltpu.SemaphoreType.DMA((SIDE + 1,)),
            pltpu.SemaphoreType.DMA((2, pairs)),
            pltpu.SemaphoreType.DMA((2, pairs)),
            pltpu.SemaphoreType.DMA((2 * pairs, 2, others, 2)),
            pltpu.SemaphoreType.DMA((2 * pairs, 2, others, 2)),
        ],
        compiler_params=pltpu.CompilerParams(
            collective_id=0, has_side_effects=True, vmem_limit_bytes=60 * 1024 * 1024
        ),
    )(level_gain, planes, weights)


def solution(mesh):
    return jax.shard_map(
        per_device,
        mesh=mesh,
        in_specs=(P("gz", None, "tile", None), P()),
        out_specs=P(None, ("tile", "gz"), None),
        check_vma=False,
    )
```

```python
import jax
import jax.numpy as jnp
import ml_dtypes
import numpy as np
from jax import lax
from jax.experimental import pallas as pl
from jax.experimental.pallas import tpu as pltpu
from jax.sharding import PartitionSpec as P

LEVELS = 4
TAPS = (0.0625, 0.25, 0.375, 0.25, 0.0625)
SIDE = 4
HALO = 32
LANES = 128
STEPS = (2, 1, 3)
CHAINS = {
    1: ((1, 16),),
    2: ((1, 17), (2, 16)),
    3: ((1, 19), (2, 18), (4, 16)),
    4: ((1, 23), (2, 22), (4, 20), (8, 16)),
}
AHEAD = 4
EXTRA = 1
UNROLL_LUM = 8
UNROLL_SCORE = 16
UNROLL_STATES = 8


def column_weights(width):
    composed = np.eye(width)
    pieces = [[], [], []]
    tails = [[], [], []]
    blocks = (0, 1, width // LANES - 1)
    for level in range(LEVELS):
        smooth = np.zeros((width, width))
        for place, factor in enumerate(TAPS):
            smooth += factor * np.eye(width, k=(place - 2) * 2**level)
        composed = smooth @ composed
        scaled = np.pad(composed / 16.0 ** (level + 1), ((0, 0), (64, 64)))
        for variant, block in enumerate(blocks):
            window = scaled[block * LANES : (block + 1) * LANES, block * LANES : block * LANES + 256].T
            head = window.astype(ml_dtypes.bfloat16)
            pieces[variant].append(head)
            if level >= 2:
                tails[variant].append((window - head.astype(np.float64)).astype(ml_dtypes.bfloat16))
    return np.stack([np.concatenate(pieces[v] + tails[v], axis=1) for v in range(3)])


def merged_states(logs, means):
    top = logs[0]
    for part in logs[1:]:
        top = jnp.maximum(top, part)
    weights = [jnp.exp(part - top) for part in logs]
    total = weights[0]
    for weight in weights[1:]:
        total = total + weight
    colours = []
    for channel in range(3):
        colour = weights[0] * means[0][channel]
        for weight, mean in zip(weights[1:], means[1:]):
            colour = colour + weight * mean[channel]
        colours.append(colour / total)
    return top, total, colours


def row_pass(source, target, stride, reach, rows, outputs, keep):
    for start in range(-reach, rows + reach, stride * outputs):
        for base in range(start, start + stride):
            at = [(base + HALO + (j - 2) * stride) * 8 for j in range(outputs + 4)]
            cells = [source[spot : spot + 8, :] for spot in at]
            for _ in range(4):
                cells = [left + right for left, right in zip(cells[:-1], cells[1:])]
            for j, cell in enumerate(cells):
                place = base + j * stride
                if place < 0:
                    cell = cell * keep[0]
                if place >= rows:
                    cell = cell * keep[1]
                target[at[j + 2] : at[j + 2] + 8, :] = cell


def focus_kernel(
    gain_ref, planes_hbm, weights_hbm, out_ref,
    planes, weights, lum, field, smooth_0, smooth_1, smooth_2, smooth_3, buf_a, buf_b, score,
    logs_zero, means_zero, logs_one, means_one, logs_two, means_two, logs_last, means_last,
    load_sems, halo_send, halo_recv, send_sems, recv_sems,
):
    smooths = (smooth_0, smooth_1, smooth_2, smooth_3)
    tile = lax.axis_index("tile")
    tiles = lax.axis_size("tile")
    place = lax.axis_index("gz")
    row = place // SIDE
    col = lax.rem(place, SIDE)
    rows = planes.shape[2]
    width = planes.shape[3]
    pairs = width // (2 * LANES)
    quarter = rows // SIDE
    extent = rows + 2 * HALO

    def peer_of(half, step):
        if half == 0:
            return lax.rem(row + step, SIDE) * SIDE + col
        return row * SIDE + lax.rem(col + step, SIDE)

    barrier = pltpu.get_barrier_semaphore()
    for half in range(2):
        for step in range(1, SIDE):
            pl.semaphore_signal(
                barrier, inc=1, device_id={"gz": peer_of(half, step)},
                device_id_type=pl.DeviceIdType.MESH,
            )

    @pl.when(tile > 0)
    def _():
        pl.semaphore_signal(
            barrier, inc=1, device_id={"tile": tile - 1}, device_id_type=pl.DeviceIdType.MESH
        )

    @pl.when(tile < tiles - 1)
    def _():
        pl.semaphore_signal(
            barrier, inc=1, device_id={"tile": tile + 1}, device_id_type=pl.DeviceIdType.MESH
        )

    loads = [
        pltpu.make_async_copy(
            planes_hbm.at[:, :, pl.ds(q * quarter, quarter), :],
            planes.at[:, :, pl.ds(q * quarter, quarter), :],
            load_sems.at[q],
        )
        for q in range(SIDE)
    ]
    weight_load = pltpu.make_async_copy(weights_hbm, weights, load_sems.at[SIDE])
    for q in (0, 3, 1, 2):
        loads[q].start()
    weight_load.start()

    def luminance(q):
        def body(index, carry):
            plane = index // 2
            start = pl.multiple_of(q * quarter + (index - plane * 2) * 16, 16)
            cells = [planes[plane, c, pl.ds(start, 16), :].astype(jnp.float32) for c in range(3)]
            value = (0.299 * cells[0] + 0.587 * cells[1] + 0.114 * cells[2]).astype(jnp.bfloat16)
            value = value.astype(jnp.float32)
            for k in range(width // LANES):
                field[k // 2, pl.ds(start * 8 + plane * 2 + k % 2, 16, stride=8), :] = value[
                    :, k * LANES : (k + 1) * LANES
                ]
            wide = jnp.concatenate([value, jnp.zeros((16, LANES), jnp.float32)], axis=1)
            wide = pltpu.roll(wide, LANES // 2, axis=1).astype(jnp.bfloat16)
            lum[plane, pl.ds(pl.multiple_of(start + HALO, 16), 16), :] = wide
            return carry

        lax.fori_loop(0, 8, body, 0, unroll=UNROLL_LUM)

    def halo_copy(side, part):
        source = HALO if side == 0 else rows
        target = HALO + rows if side == 0 else 0
        peer = tile - 1 if side == 0 else tile + 1
        first = 0 if part == 0 else (2 * part + 1) * LANES
        lanes = pl.ds(first, (2 * part + 3) * LANES - first)
        return pltpu.make_async_remote_copy(
            src_ref=lum.at[:, pl.ds(source, HALO), lanes],
            dst_ref=lum.at[:, pl.ds(target, HALO), lanes],
            send_sem=halo_send.at[side, part], recv_sem=halo_recv.at[side, part],
            device_id={"tile": peer}, device_id_type=pl.DeviceIdType.MESH,
        )

    loads[0].wait()
    luminance(0)
    neighbours = jnp.where(tile > 0, 1, 0) + jnp.where(tile < tiles - 1, 1, 0)
    pl.semaphore_wait(barrier, 2 * (SIDE - 1) + neighbours)

    @pl.when(tile > 0)
    def _():
        for part in range(pairs):
            halo_copy(0, part).start()

    @pl.when(tile == 0)
    def _():
        lum[:, 0:HALO, :] = jnp.zeros((SIDE, HALO, width + LANES), jnp.bfloat16)

    loads[3].wait()
    luminance(3)

    @pl.when(tile < tiles - 1)
    def _():
        for part in range(pairs):
            halo_copy(1, part).start()

    @pl.when(tile == tiles - 1)
    def _():
        lum[:, HALO + rows : extent, :] = jnp.zeros((SIDE, HALO, width + LANES), jnp.bfloat16)

    for q in (1, 2):
        loads[q].wait()
        luminance(q)
    weight_load.wait()

    def columns(pair, spans):
        for k in range(2):
            block = pair * 2 + k
            variant = 0 if block == 0 else 2 if block == 2 * pairs - 1 else 1
            window = pl.ds(block * LANES, 2 * LANES)
            smooth = smooths[pair]
            cells = jnp.concatenate(
                [
                    lum[plane, start : start + count, window]
                    for plane in range(SIDE)
                    for start, count in spans
                ],
                axis=0,
            )
            low = jnp.dot(cells, weights[variant, :, 0:256], preferred_element_type=jnp.float32)
            high = jnp.dot(
                jnp.concatenate([cells, cells], axis=1),
                jnp.concatenate([weights[variant, :, 256:512], weights[variant, :, 512:768]], axis=0),
                preferred_element_type=jnp.float32,
            )
            at = 0
            for plane in range(SIDE):
                for start, count in spans:
                    spot = pl.ds(start * 8 + plane * 2 + k, count, stride=8)
                    part = slice(at, at + count)
                    smooth[0, spot, :] = low[part, :LANES]
                    smooth[1, spot, :] = low[part, LANES:]
                    smooth[2, spot, :] = high[part, :LANES]
                    smooth[3, spot, :] = high[part, LANES:]
                    at += count

    inner = ((HALO, rows),)
    outer = ((0, HALO), (HALO + rows, HALO))
    for pair in range(AHEAD):
        columns(pair, inner)

    def outer_columns(pair):
        @pl.when(tile < tiles - 1)
        def _():
            halo_copy(0, pair).wait_recv()

        @pl.when(tile > 0)
        def _():
            halo_copy(1, pair).wait_recv()

        columns(pair, outer)

    keep = (jnp.where(tile == 0, 0.0, 1.0), jnp.where(tile == tiles - 1, 0.0, 1.0))

    def rows_smoothed(pair):
        for level in range(LEVELS, 0, -1):
            chain = CHAINS[level]
            reach = sum(2 * stride for stride, _ in chain)
            own = smooths[pair].at[level - 1]
            source = own
            for index, (stride, outputs) in enumerate(chain):
                reach -= 2 * stride
                target = (buf_a, buf_b)[index % 2]
                if index == level - 1 and level > 1:
                    target = own
                row_pass(source, target, stride, reach, rows, outputs, keep)
                source = target

    gains = [gain_ref[level] for level in range(LEVELS)]

    def scored(pair):
        def body(block, carry):
            here = pl.ds(pl.multiple_of(block * 64, 64), 64)
            wide = pl.ds(pl.multiple_of(block * 64 + HALO * 8, 64), 64)
            approx = [field[pair, here, :], buf_a[wide, :]]
            approx += [smooths[pair][level, wide, :] for level in range(1, LEVELS)]
            energy = None
            for level in range(LEVELS):
                detail = approx[level] - approx[level + 1]
                term = gains[level] * (detail * detail)
                energy = term if energy is None else energy + term
            score[here, :] = energy
            return carry

        lax.fori_loop(0, rows // 8, body, 0, unroll=UNROLL_SCORE)

    def states(pair, k):
        def body(block, carry):
            here = pl.ds(pl.multiple_of(block * 16, 16), 16)
            far = block // 2
            near = (block - far * 2) * 2
            lanes = pl.ds(pl.multiple_of((pair * 2 + k) * LANES, LANES), LANES)
            parts = [
                score[pl.ds(block * 128 + plane * 2 + k, 16, stride=8), :] for plane in range(SIDE)
            ]
            top = jnp.maximum(jnp.maximum(parts[0], parts[1]), jnp.maximum(parts[2], parts[3]))
            shares = [jnp.exp(part - top) for part in parts]
            total = (shares[0] + shares[1]) + (shares[2] + shares[3])
            inverse = 1.0 / total
            shares = [share * inverse for share in shares]
            log_sum = top + jnp.log(total)
            spots = ((far, near), (far, near + 1)) if k == 0 else ((near, far), (near + 1, far))
            for part, (first, second) in enumerate(spots):
                logs_zero[pair, k, first, second] = log_sum[part * 8 : part * 8 + 8]
            for channel in range(3):
                mean = shares[0] * planes[0, channel, here, lanes].astype(jnp.float32)
                for plane in range(1, SIDE):
                    mean = mean + shares[plane] * planes[plane, channel, here, lanes].astype(
                        jnp.float32
                    )
                mean = mean.astype(jnp.bfloat16)
                for part, (first, second) in enumerate(spots):
                    means_zero[pair, k, first, second, channel] = mean[part * 8 : part * 8 + 8]
            return carry

        lax.fori_loop(0, rows // 16, body, 0, unroll=UNROLL_STATES)

    def first_copies(pair, half, step):
        index = lax.rem((row if half == 0 else col) + step, SIDE)
        return [
            pltpu.make_async_remote_copy(
                src_ref=source.at[pair, half, index], dst_ref=target.at[pair, half, step - 1],
                send_sem=send_sems.at[pair, half, step - 1, kind],
                recv_sem=recv_sems.at[pair, half, step - 1, kind],
                device_id={"gz": peer_of(half, step)}, device_id_type=pl.DeviceIdType.MESH,
            )
            for kind, (source, target) in enumerate(
                ((logs_zero, logs_one), (means_zero, means_one))
            )
        ]

    def first_merge(pair, half):
        own = row if half == 0 else col
        for step in STEPS:
            for copy in first_copies(pair, half, step):
                copy.wait_recv()

        for second in range(SIDE):
            logs = [logs_zero[pair, half, own, second]]
            logs += [logs_one[pair, half, k, second] for k in range(SIDE - 1)]
            means = [means_zero[pair, half, own, second].astype(jnp.float32)]
            means += [
                means_one[pair, half, k, second].astype(jnp.float32) for k in range(SIDE - 1)
            ]
            top, total, colours = merged_states(logs, means)
            logs_two[pair, half, second] = top + jnp.log(total)
            for channel in range(3):
                means_two[pair, half, second, channel] = colours[channel].astype(jnp.bfloat16)

    def one_pair(pair):
        if pair > 0:
            if AHEAD <= pair + EXTRA < pairs:
                columns(pair + EXTRA, inner)
            outer_columns(pair)
        rows_smoothed(pair)
        scored(pair)
        for half in range(2):
            states(pair, half)
            for step in STEPS:
                for copy in first_copies(pair, half, step):
                    copy.start()

        if pair > 1:
            advance(pair - 2)

    def advance(pair):
        for half in range(2):
            first_merge(pair, half)
            for step in STEPS:
                for copy in last_copies(pair, half, step):
                    copy.start()

    def last_copies(pair, half, step):
        index = lax.rem((col if half == 0 else row) + step, SIDE)
        return [
            pltpu.make_async_remote_copy(
                src_ref=source.at[pair, half, index], dst_ref=target.at[pair, half, step - 1],
                send_sem=send_sems.at[pairs + pair, half, step - 1, kind],
                recv_sem=recv_sems.at[pairs + pair, half, step - 1, kind],
                device_id={"gz": peer_of(1 - half, step)}, device_id_type=pl.DeviceIdType.MESH,
            )
            for kind, (source, target) in enumerate(((logs_two, logs_last), (means_two, means_last)))
        ]

    def last_merge(pair):
        for half in range(2):
            own = col if half == 0 else row
            for step in STEPS:
                for copy in last_copies(pair, half, step):
                    copy.wait_recv()
            logs = [logs_two[pair, half, own]] + [logs_last[pair, half, k] for k in range(SIDE - 1)]
            means = [means_two[pair, half, own].astype(jnp.float32)]
            means += [means_last[pair, half, k].astype(jnp.float32) for k in range(SIDE - 1)]
            _, _, colours = merged_states(logs, means)
            lanes = slice((pair * 2 + half) * LANES, (pair * 2 + half + 1) * LANES)
            for channel in range(3):
                out_ref[channel, :, lanes] = colours[channel].astype(jnp.bfloat16)

    outer_columns(0)
    for pair in range(pairs):
        one_pair(pair)
    advance(pairs - 2)
    advance(pairs - 1)
    for pair in range(pairs):
        last_merge(pair)

    @pl.when(tile > 0)
    def _():
        for part in range(pairs):
            halo_copy(0, part).wait_send()

    @pl.when(tile < tiles - 1)
    def _():
        for part in range(pairs):
            halo_copy(1, part).wait_send()

    def drain(pair, carry):
        for half in range(2):
            for step in STEPS:
                for copy in first_copies(pair, half, step) + last_copies(pair, half, step):
                    copy.wait_send()
        return carry

    lax.fori_loop(0, pairs, drain, 0)


def per_device(planes, level_gain):
    _, channels, rows, width = planes.shape
    share = rows // (SIDE * SIDE)
    pairs = width // (2 * LANES)
    extent = rows + 2 * HALO
    weights = jnp.asarray(column_weights(width))
    others = SIDE - 1
    return pl.pallas_call(
        focus_kernel,
        out_shape=jax.ShapeDtypeStruct((channels, share, width), jnp.bfloat16),
        in_specs=[
            pl.BlockSpec(memory_space=pltpu.SMEM),
            pl.BlockSpec(memory_space=pl.ANY),
            pl.BlockSpec(memory_space=pl.ANY),
        ],
        out_specs=pl.BlockSpec(memory_space=pltpu.VMEM),
        scratch_shapes=[
            pltpu.VMEM(planes.shape, jnp.bfloat16),
            pltpu.VMEM(weights.shape, jnp.bfloat16),
            pltpu.VMEM((SIDE, extent, width + LANES), jnp.bfloat16),
            pltpu.VMEM((pairs, rows * 8, LANES), jnp.float32),
            pltpu.VMEM((LEVELS, extent * 8, LANES), jnp.float32),
            pltpu.VMEM((LEVELS, extent * 8, LANES), jnp.float32),
            pltpu.VMEM((LEVELS, extent * 8, LANES), jnp.float32),
            pltpu.VMEM((LEVELS, extent * 8, LANES), jnp.float32),
            pltpu.VMEM((extent * 8, LANES), jnp.float32),
            pltpu.VMEM((extent * 8, LANES), jnp.float32),
            pltpu.VMEM((rows * 8, LANES), jnp.float32),
            pltpu.VMEM((pairs, 2, SIDE, SIDE, share, LANES), jnp.float32),
            pltpu.VMEM((pairs, 2, SIDE, SIDE, channels, share, LANES), jnp.bfloat16),
            pltpu.VMEM((pairs, 2, others, SIDE, share, LANES), jnp.float32),
            pltpu.VMEM((pairs, 2, others, SIDE, channels, share, LANES), jnp.bfloat16),
            pltpu.VMEM((pairs, 2, SIDE, share, LANES), jnp.float32),
            pltpu.VMEM((pairs, 2, SIDE, channels, share, LANES), jnp.bfloat16),
            pltpu.VMEM((pairs, 2, others, share, LANES), jnp.float32),
            pltpu.VMEM((pairs, 2, others, channels, share, LANES), jnp.bfloat16),
            pltpu.SemaphoreType.DMA((SIDE + 1,)),
            pltpu.SemaphoreType.DMA((2, pairs)),
            pltpu.SemaphoreType.DMA((2, pairs)),
            pltpu.SemaphoreType.DMA((2 * pairs, 2, others, 2)),
            pltpu.SemaphoreType.DMA((2 * pairs, 2, others, 2)),
        ],
        compiler_params=pltpu.CompilerParams(
            collective_id=0, has_side_effects=True, vmem_limit_bytes=60 * 1024 * 1024
        ),
    )(level_gain, planes, weights)


def solution(mesh):
    return jax.shard_map(
        per_device,
        mesh=mesh,
        in_specs=(P("gz", None, "tile", None), P()),
        out_specs=P(None, ("tile", "gz"), None),
        check_vma=False,
    )
```

```python
import jax
import jax.numpy as jnp
import ml_dtypes
import numpy as np
from jax import lax
from jax.experimental import pallas as pl
from jax.experimental.pallas import tpu as pltpu
from jax.sharding import PartitionSpec as P

LEVELS = 4
TAPS = (0.0625, 0.25, 0.375, 0.25, 0.0625)
SIDE = 4
HALO = 32
LANES = 128
STEPS = (2, 1, 3)
CHAINS = {
    1: ((1, 16),),
    2: ((1, 17), (2, 16)),
    3: ((1, 19), (2, 18), (4, 16)),
    4: ((1, 23), (2, 22), (4, 20), (8, 16)),
}
AHEAD = 4
EXTRA = 1
UNROLL_LUM = 8
UNROLL_SCORE = 16
UNROLL_STATES = 8


def column_weights(width):
    composed = np.eye(width)
    pieces = [[], [], []]
    tails = [[], [], []]
    blocks = (0, 1, width // LANES - 1)
    for level in range(LEVELS):
        smooth = np.zeros((width, width))
        for place, factor in enumerate(TAPS):
            smooth += factor * np.eye(width, k=(place - 2) * 2**level)
        composed = smooth @ composed
        scaled = np.pad(composed / 16.0 ** (level + 1), ((0, 0), (64, 64)))
        for variant, block in enumerate(blocks):
            window = scaled[block * LANES : (block + 1) * LANES, block * LANES : block * LANES + 256].T
            head = window.astype(ml_dtypes.bfloat16)
            pieces[variant].append(head)
            if level >= 2:
                tails[variant].append((window - head.astype(np.float64)).astype(ml_dtypes.bfloat16))
    return np.stack([np.concatenate(pieces[v] + tails[v], axis=1) for v in range(3)])


def merged_states(logs, means):
    top = logs[0]
    for part in logs[1:]:
        top = jnp.maximum(top, part)
    weights = [jnp.exp(part - top) for part in logs]
    total = weights[0]
    for weight in weights[1:]:
        total = total + weight
    colours = []
    for channel in range(3):
        colour = weights[0] * means[0][channel]
        for weight, mean in zip(weights[1:], means[1:]):
            colour = colour + weight * mean[channel]
        colours.append(colour / total)
    return top, total, colours


def row_pass(source, target, stride, reach, rows, outputs, keep):
    for start in range(-reach, rows + reach, stride * outputs):
        for base in range(start, start + stride):
            at = [(base + HALO + (j - 2) * stride) * 8 for j in range(outputs + 4)]
            cells = [source[spot : spot + 8, :] for spot in at]
            for _ in range(4):
                cells = [left + right for left, right in zip(cells[:-1], cells[1:])]
            for j, cell in enumerate(cells):
                place = base + j * stride
                if place < 0:
                    cell = cell * keep[0]
                if place >= rows:
                    cell = cell * keep[1]
                target[at[j + 2] : at[j + 2] + 8, :] = cell


def focus_kernel(
    gain_ref, planes_hbm, weights_hbm, out_ref,
    planes, weights, lum, field, smooth_0, smooth_1, smooth_2, smooth_3, buf_a, buf_b, score,
    logs_zero, means_zero, logs_one, means_one, logs_two, means_two, logs_last, means_last,
    load_sems, halo_send, halo_recv, send_sems, recv_sems,
):
    smooths = (smooth_0, smooth_1, smooth_2, smooth_3)
    tile = lax.axis_index("tile")
    tiles = lax.axis_size("tile")
    place = lax.axis_index("gz")
    row = place // SIDE
    col = lax.rem(place, SIDE)
    rows = planes.shape[2]
    width = planes.shape[3]
    pairs = width // (2 * LANES)
    quarter = rows // SIDE
    extent = rows + 2 * HALO

    def peer_of(half, step):
        if half == 0:
            return lax.rem(row + step, SIDE) * SIDE + col
        return row * SIDE + lax.rem(col + step, SIDE)

    barrier = pltpu.get_barrier_semaphore()
    for half in range(2):
        for step in range(1, SIDE):
            pl.semaphore_signal(
                barrier, inc=1, device_id={"gz": peer_of(half, step)},
                device_id_type=pl.DeviceIdType.MESH,
            )

    @pl.when(tile > 0)
    def _():
        pl.semaphore_signal(
            barrier, inc=1, device_id={"tile": tile - 1}, device_id_type=pl.DeviceIdType.MESH
        )

    @pl.when(tile < tiles - 1)
    def _():
        pl.semaphore_signal(
            barrier, inc=1, device_id={"tile": tile + 1}, device_id_type=pl.DeviceIdType.MESH
        )

    loads = [
        pltpu.make_async_copy(
            planes_hbm.at[:, :, pl.ds(q * quarter, quarter), :],
            planes.at[:, :, pl.ds(q * quarter, quarter), :],
            load_sems.at[q],
        )
        for q in range(SIDE)
    ]
    weight_load = pltpu.make_async_copy(weights_hbm, weights, load_sems.at[SIDE])
    for q in (0, 3, 1, 2):
        loads[q].start()
    weight_load.start()

    def luminance(q):
        def body(index, carry):
            plane = index // 2
            start = pl.multiple_of(q * quarter + (index - plane * 2) * 16, 16)
            cells = [planes[plane, c, pl.ds(start, 16), :].astype(jnp.float32) for c in range(3)]
            value = (0.299 * cells[0] + 0.587 * cells[1] + 0.114 * cells[2]).astype(jnp.bfloat16)
            value = value.astype(jnp.float32)
            for k in range(width // LANES):
                field[k // 2, pl.ds(start * 8 + plane * 2 + k % 2, 16, stride=8), :] = value[
                    :, k * LANES : (k + 1) * LANES
                ]
            wide = jnp.concatenate([value, jnp.zeros((16, LANES), jnp.float32)], axis=1)
            wide = pltpu.roll(wide, LANES // 2, axis=1).astype(jnp.bfloat16)
            lum[plane, pl.ds(pl.multiple_of(start + HALO, 16), 16), :] = wide
            return carry

        lax.fori_loop(0, 8, body, 0, unroll=UNROLL_LUM)

    def halo_copy(side, part):
        source = HALO if side == 0 else rows
        target = HALO + rows if side == 0 else 0
        peer = tile - 1 if side == 0 else tile + 1
        first = 0 if part == 0 else (2 * part + 1) * LANES
        lanes = pl.ds(first, (2 * part + 3) * LANES - first)
        return pltpu.make_async_remote_copy(
            src_ref=lum.at[:, pl.ds(source, HALO), lanes],
            dst_ref=lum.at[:, pl.ds(target, HALO), lanes],
            send_sem=halo_send.at[side, part], recv_sem=halo_recv.at[side, part],
            device_id={"tile": peer}, device_id_type=pl.DeviceIdType.MESH,
        )

    loads[0].wait()
    luminance(0)
    neighbours = jnp.where(tile > 0, 1, 0) + jnp.where(tile < tiles - 1, 1, 0)
    pl.semaphore_wait(barrier, 2 * (SIDE - 1) + neighbours)

    @pl.when(tile > 0)
    def _():
        halo_copy(0, 0).start()

    @pl.when(tile == 0)
    def _():
        lum[:, 0:HALO, :] = jnp.zeros((SIDE, HALO, width + LANES), jnp.bfloat16)

    loads[3].wait()
    luminance(3)

    @pl.when(tile < tiles - 1)
    def _():
        halo_copy(1, 0).start()

    @pl.when(tile == tiles - 1)
    def _():
        lum[:, HALO + rows : extent, :] = jnp.zeros((SIDE, HALO, width + LANES), jnp.bfloat16)

    @pl.when(tile > 0)
    def _():
        for part in range(1, pairs):
            halo_copy(0, part).start()

    @pl.when(tile < tiles - 1)
    def _():
        for part in range(1, pairs):
            halo_copy(1, part).start()

    for q in (1, 2):
        loads[q].wait()
        luminance(q)
    weight_load.wait()

    def columns(pair, spans):
        for k in range(2):
            block = pair * 2 + k
            variant = 0 if block == 0 else 2 if block == 2 * pairs - 1 else 1
            window = pl.ds(block * LANES, 2 * LANES)
            smooth = smooths[pair]
            cells = jnp.concatenate(
                [
                    lum[plane, start : start + count, window]
                    for plane in range(SIDE)
                    for start, count in spans
                ],
                axis=0,
            )
            low = jnp.dot(cells, weights[variant, :, 0:256], preferred_element_type=jnp.float32)
            high = jnp.dot(
                jnp.concatenate([cells, cells], axis=1),
                jnp.concatenate([weights[variant, :, 256:512], weights[variant, :, 512:768]], axis=0),
                preferred_element_type=jnp.float32,
            )
            at = 0
            for plane in range(SIDE):
                for start, count in spans:
                    spot = pl.ds(start * 8 + plane * 2 + k, count, stride=8)
                    part = slice(at, at + count)
                    smooth[0, spot, :] = low[part, :LANES]
                    smooth[1, spot, :] = low[part, LANES:]
                    smooth[2, spot, :] = high[part, :LANES]
                    smooth[3, spot, :] = high[part, LANES:]
                    at += count

    inner = ((HALO, rows),)
    outer = ((0, HALO), (HALO + rows, HALO))
    for pair in range(AHEAD):
        columns(pair, inner)

    def outer_columns(pair):
        @pl.when(tile < tiles - 1)
        def _():
            halo_copy(0, pair).wait_recv()

        @pl.when(tile > 0)
        def _():
            halo_copy(1, pair).wait_recv()

        columns(pair, outer)

    keep = (jnp.where(tile == 0, 0.0, 1.0), jnp.where(tile == tiles - 1, 0.0, 1.0))

    def rows_smoothed(pair):
        for level in range(LEVELS, 0, -1):
            chain = CHAINS[level]
            reach = sum(2 * stride for stride, _ in chain)
            own = smooths[pair].at[level - 1]
            source = own
            for index, (stride, outputs) in enumerate(chain):
                reach -= 2 * stride
                target = (buf_a, buf_b)[index % 2]
                if index == level - 1 and level > 1:
                    target = own
                row_pass(source, target, stride, reach, rows, outputs, keep)
                source = target

    gains = [gain_ref[level] for level in range(LEVELS)]

    def scored(pair):
        def body(block, carry):
            here = pl.ds(pl.multiple_of(block * 64, 64), 64)
            wide = pl.ds(pl.multiple_of(block * 64 + HALO * 8, 64), 64)
            approx = [field[pair, here, :], buf_a[wide, :]]
            approx += [smooths[pair][level, wide, :] for level in range(1, LEVELS)]
            energy = None
            for level in range(LEVELS):
                detail = approx[level] - approx[level + 1]
                term = gains[level] * (detail * detail)
                energy = term if energy is None else energy + term
            score[here, :] = energy
            return carry

        lax.fori_loop(0, rows // 8, body, 0, unroll=UNROLL_SCORE)

    def states(pair, k):
        def body(block, carry):
            here = pl.ds(pl.multiple_of(block * 16, 16), 16)
            far = block // 2
            near = (block - far * 2) * 2
            lanes = pl.ds(pl.multiple_of((pair * 2 + k) * LANES, LANES), LANES)
            parts = [
                score[pl.ds(block * 128 + plane * 2 + k, 16, stride=8), :] for plane in range(SIDE)
            ]
            top = jnp.maximum(jnp.maximum(parts[0], parts[1]), jnp.maximum(parts[2], parts[3]))
            shares = [jnp.exp(part - top) for part in parts]
            total = (shares[0] + shares[1]) + (shares[2] + shares[3])
            inverse = 1.0 / total
            shares = [share * inverse for share in shares]
            log_sum = top + jnp.log(total)
            spots = ((far, near), (far, near + 1)) if k == 0 else ((near, far), (near + 1, far))
            for part, (first, second) in enumerate(spots):
                logs_zero[pair, k, first, second] = log_sum[part * 8 : part * 8 + 8]
            for channel in range(3):
                mean = shares[0] * planes[0, channel, here, lanes].astype(jnp.float32)
                for plane in range(1, SIDE):
                    mean = mean + shares[plane] * planes[plane, channel, here, lanes].astype(
                        jnp.float32
                    )
                mean = mean.astype(jnp.bfloat16)
                for part, (first, second) in enumerate(spots):
                    means_zero[pair, k, first, second, channel] = mean[part * 8 : part * 8 + 8]
            return carry

        lax.fori_loop(0, rows // 16, body, 0, unroll=UNROLL_STATES)

    def first_copies(pair, half, step):
        index = lax.rem((row if half == 0 else col) + step, SIDE)
        return [
            pltpu.make_async_remote_copy(
                src_ref=source.at[pair, half, index], dst_ref=target.at[pair, half, step - 1],
                send_sem=send_sems.at[pair, half, step - 1, kind],
                recv_sem=recv_sems.at[pair, half, step - 1, kind],
                device_id={"gz": peer_of(half, step)}, device_id_type=pl.DeviceIdType.MESH,
            )
            for kind, (source, target) in enumerate(
                ((logs_zero, logs_one), (means_zero, means_one))
            )
        ]

    def first_merge(pair, half):
        own = row if half == 0 else col
        for step in STEPS:
            for copy in first_copies(pair, half, step):
                copy.wait_recv()

        for second in range(SIDE):
            logs = [logs_zero[pair, half, own, second]]
            logs += [logs_one[pair, half, k, second] for k in range(SIDE - 1)]
            means = [means_zero[pair, half, own, second].astype(jnp.float32)]
            means += [
                means_one[pair, half, k, second].astype(jnp.float32) for k in range(SIDE - 1)
            ]
            top, total, colours = merged_states(logs, means)
            logs_two[pair, half, second] = top + jnp.log(total)
            for channel in range(3):
                means_two[pair, half, second, channel] = colours[channel].astype(jnp.bfloat16)

    def one_pair(pair):
        if pair > 0:
            if AHEAD <= pair + EXTRA < pairs:
                columns(pair + EXTRA, inner)
            outer_columns(pair)
        rows_smoothed(pair)
        scored(pair)
        for half in range(2):
            states(pair, half)
            for step in STEPS:
                for copy in first_copies(pair, half, step):
                    copy.start()

        if pair > 1:
            advance(pair - 2)

    def advance(pair):
        for half in range(2):
            first_merge(pair, half)
            for step in STEPS:
                for copy in last_copies(pair, half, step):
                    copy.start()

    def last_copies(pair, half, step):
        index = lax.rem((col if half == 0 else row) + step, SIDE)
        return [
            pltpu.make_async_remote_copy(
                src_ref=source.at[pair, half, index], dst_ref=target.at[pair, half, step - 1],
                send_sem=send_sems.at[pairs + pair, half, step - 1, kind],
                recv_sem=recv_sems.at[pairs + pair, half, step - 1, kind],
                device_id={"gz": peer_of(1 - half, step)}, device_id_type=pl.DeviceIdType.MESH,
            )
            for kind, (source, target) in enumerate(((logs_two, logs_last), (means_two, means_last)))
        ]

    def last_merge(pair):
        for half in range(2):
            own = col if half == 0 else row
            for step in STEPS:
                for copy in last_copies(pair, half, step):
                    copy.wait_recv()
            logs = [logs_two[pair, half, own]] + [logs_last[pair, half, k] for k in range(SIDE - 1)]
            means = [means_two[pair, half, own].astype(jnp.float32)]
            means += [means_last[pair, half, k].astype(jnp.float32) for k in range(SIDE - 1)]
            _, _, colours = merged_states(logs, means)
            lanes = slice((pair * 2 + half) * LANES, (pair * 2 + half + 1) * LANES)
            for channel in range(3):
                out_ref[channel, :, lanes] = colours[channel].astype(jnp.bfloat16)

    outer_columns(0)
    for pair in range(pairs):
        one_pair(pair)
    def drain_first(pair):
        for half in range(2):
            for step in STEPS:
                for copy in first_copies(pair, half, step):
                    copy.wait_send()

    def drain_last(pair):
        for half in range(2):
            for step in STEPS:
                for copy in last_copies(pair, half, step):
                    copy.wait_send()

    advance(pairs - 2)
    for pair in range(pairs - 1):
        drain_first(pair)
    last_merge(0)
    advance(pairs - 1)

    @pl.when(tile > 0)
    def _():
        for part in range(pairs):
            halo_copy(0, part).wait_send()

    @pl.when(tile < tiles - 1)
    def _():
        for part in range(pairs):
            halo_copy(1, part).wait_send()

    drain_first(pairs - 1)
    for pair in range(pairs - 1):
        drain_last(pair)
    for pair in range(1, pairs):
        last_merge(pair)
    drain_last(pairs - 1)


def per_device(planes, level_gain):
    _, channels, rows, width = planes.shape
    share = rows // (SIDE * SIDE)
    pairs = width // (2 * LANES)
    extent = rows + 2 * HALO
    weights = jnp.asarray(column_weights(width))
    others = SIDE - 1
    return pl.pallas_call(
        focus_kernel,
        out_shape=jax.ShapeDtypeStruct((channels, share, width), jnp.bfloat16),
        in_specs=[
            pl.BlockSpec(memory_space=pltpu.SMEM),
            pl.BlockSpec(memory_space=pl.ANY),
            pl.BlockSpec(memory_space=pl.ANY),
        ],
        out_specs=pl.BlockSpec(memory_space=pltpu.VMEM),
        scratch_shapes=[
            pltpu.VMEM(planes.shape, jnp.bfloat16),
            pltpu.VMEM(weights.shape, jnp.bfloat16),
            pltpu.VMEM((SIDE, extent, width + LANES), jnp.bfloat16),
            pltpu.VMEM((pairs, rows * 8, LANES), jnp.float32),
            pltpu.VMEM((LEVELS, extent * 8, LANES), jnp.float32),
            pltpu.VMEM((LEVELS, extent * 8, LANES), jnp.float32),
            pltpu.VMEM((LEVELS, extent * 8, LANES), jnp.float32),
            pltpu.VMEM((LEVELS, extent * 8, LANES), jnp.float32),
            pltpu.VMEM((extent * 8, LANES), jnp.float32),
            pltpu.VMEM((extent * 8, LANES), jnp.float32),
            pltpu.VMEM((rows * 8, LANES), jnp.float32),
            pltpu.VMEM((pairs, 2, SIDE, SIDE, share, LANES), jnp.float32),
            pltpu.VMEM((pairs, 2, SIDE, SIDE, channels, share, LANES), jnp.bfloat16),
            pltpu.VMEM((pairs, 2, others, SIDE, share, LANES), jnp.float32),
            pltpu.VMEM((pairs, 2, others, SIDE, channels, share, LANES), jnp.bfloat16),
            pltpu.VMEM((pairs, 2, SIDE, share, LANES), jnp.float32),
            pltpu.VMEM((pairs, 2, SIDE, channels, share, LANES), jnp.bfloat16),
            pltpu.VMEM((pairs, 2, others, share, LANES), jnp.float32),
            pltpu.VMEM((pairs, 2, others, channels, share, LANES), jnp.bfloat16),
            pltpu.SemaphoreType.DMA((SIDE + 1,)),
            pltpu.SemaphoreType.DMA((2, pairs)),
            pltpu.SemaphoreType.DMA((2, pairs)),
            pltpu.SemaphoreType.DMA((2 * pairs, 2, others, 2)),
            pltpu.SemaphoreType.DMA((2 * pairs, 2, others, 2)),
        ],
        compiler_params=pltpu.CompilerParams(
            collective_id=0, has_side_effects=True, vmem_limit_bytes=60 * 1024 * 1024
        ),
    )(level_gain, planes, weights)


def solution(mesh):
    return jax.shard_map(
        per_device,
        mesh=mesh,
        in_specs=(P("gz", None, "tile", None), P()),
        out_specs=P(None, ("tile", "gz"), None),
        check_vma=False,
    )
```
